512 devices in a mesh: space: 64 (over z, y_lo, core), kgrp: 8 (over y_hi, x).
Axes of the slice: x: 4, y: 4 (y_hi: 2, y_lo: 2; y = y_hi * 2 + y_lo), z: 16, core: 2. Of those that a mesh axis runs over, the one named last changes fastest.
Arguments:
- features: bfloat16 [65536, 128], P(('space', 'kgrp')), may hold values from -8 to 8, as said below
- positions: float32 [65536, 3], P('space'), may hold values from 0 to 8192, as said below
- wave_index: int32 [6144, 3], P('kgrp'), may hold values from -12 to 12, as said below
- wave_filter: float32 [6144, 128], P('kgrp'), may hold values from 0.2 to 2
- mix_pair: bfloat16 [2, 128, 128], replicated, may hold values from -0.5 to 0.5
- msg_weight: bfloat16 [128, 128], replicated, may hold values from -0.5 to 0.5
- chan_width: float32 [128], replicated, may hold values from 1 to 30
- pair_dist: float32 [65536, 16], P(('space', 'kgrp')), may hold values from 1 to 25
- neighbours: int32 [65536, 16], P(('space', 'kgrp')), may hold values from 0 to 191, as said below
- norm_gain: float32 [128], replicated, may hold values from 0.1 to 1.9
- in_weight: bfloat16 [128, 512], replicated, may hold values from -0.5 to 0.5
- out_weight: bfloat16 [512, 128], replicated, may hold values from -0.25 to 0.25
Outputs:
- updated: bfloat16 [65536, 128], P(('space', 'kgrp'))
The draws below stay inside these ranges and needn't reach their ends.
Inputs may be any that keep to these rules, and one draw needn't show every extreme that they name: Entries of the features are clipped to the range. `positions`: x and y lie in [0, 16); atom i has z in [i / 8, (i + 1) / 8). `wave_index`: the wave vectors are distinct and nonzero, one of each plus-minus k pair: each is lexicographically positive (first nonzero component positive). Rows of a device's extended block are its lower 32 wrapped neighbours' rows, its own 128 rows, then 32 upper ones; an atom at own row r lists rows r + 32 + o with 1 <= |o| <= 32.
All inputs are finite; a program needn't handle non-finite values.
Results may differ from the reference program's by a relative error of at most 0.008.
Values may be sent and summed in bfloat16 or wider, within the bound.
A program may use at most 64 MiB of HBM per device.

```python
import math
import jax
import jax.numpy as jnp
from jax import lax

F = 128
H = 512
NB = 16
KMAX = 12
ATOM_DEV = 128
ATOMS = 65536
WAVES = 6144
N_SPACE = 64
N_KGRP = 8


def draw_features(key, part):
    key_base, key_rows, key_cols = jax.random.split(key, 3)
    row_scale = jnp.exp(jax.random.uniform(key_rows, (ATOMS, 1), minval=math.log(0.3), maxval=math.log(3.0)))
    col_scale = jnp.exp(jax.random.uniform(key_cols, (1, F), minval=math.log(0.5), maxval=math.log(2.0)))
    base = jax.random.normal(key_base, (ATOMS, F))
    return jnp.clip(base * row_scale * col_scale, -8.0, 8.0).astype(jnp.bfloat16)


def draw_positions(key, part):
    key_plane, key_depth = jax.random.split(key, 2)
    plane = jax.random.uniform(key_plane, (ATOMS, 2), minval=0.0, maxval=16.0)
    order = jnp.arange(ATOMS, dtype=jnp.int32).astype(jnp.float32)
    depth = (order + jax.random.uniform(key_depth, (ATOMS,), minval=0.0, maxval=0.999)) * 0.125
    return jnp.concatenate([plane, depth[:, None]], axis=1).astype(jnp.float32)


def draw_wave_index(key, part):
    side = 2 * KMAX + 1
    centre = (side * side * side - 1) // 2
    chosen = jax.random.permutation(jax.random.fold_in(key, 71), centre)[:WAVES].astype(jnp.int32) + centre + 1
    first = chosen // (side * side) - KMAX
    second = chosen // side % side - KMAX
    third = chosen % side - KMAX
    return jnp.stack([first, second, third], axis=1).astype(jnp.int32)


def draw_neighbours(key, part):
    halo_width = ATOM_DEV // 4
    key_reach, key_side = jax.random.split(key, 2)
    reach = jax.random.randint(key_reach, (ATOMS, NB), 1, halo_width + 1)
    side = jax.random.randint(key_side, (ATOMS, NB), 0, 2) * 2 - 1
    offset = reach * side
    local = (jnp.arange(ATOMS, dtype=jnp.int32) % ATOM_DEV)[:, None]
    slot = jnp.arange(NB, dtype=jnp.int32)[None, :]
    offset = jnp.where((local == 0) & (slot == 0), -halo_width, offset)
    offset = jnp.where((local == ATOM_DEV - 1) & (slot == 0), halo_width, offset)
    return (local + halo_width + offset).astype(jnp.int32)


def levels(stream_key, extent, pieces, low, top_value):
    def one(position, shards_of):
        draws = jax.random.uniform(jax.random.fold_in(jax.random.fold_in(stream_key, 6), position), (shards_of,), jnp.float32, low / len(pieces), top_value / len(pieces))
        return jnp.repeat(jnp.exp(draws), extent[position] // shards_of).reshape((-1,) + (1,) * (len(extent) - position - 1))

    factor_of = one(*pieces[0])
    for cut in pieces[1:]:
        factor_of = factor_of * one(*cut)
    return factor_of


def scatter_about(own_key, shape, deviation, bound, held_as=jnp.bfloat16):
    values = deviation * jax.random.normal(own_key, shape, jnp.float32)
    return jnp.clip(values, min=-bound, max=bound).astype(held_as)


def setup_inputs(seed: int = 0) -> dict:
    seeds = jax.random.split(jax.random.key(seed), 13)
    return {
        "features": draw_features(jax.random.fold_in(seeds[12], 71), 0),
        "positions": draw_positions(jax.random.fold_in(seeds[12], 71), 0),
        "wave_index": draw_wave_index(jax.random.fold_in(seeds[12], 71), 0),
        "wave_filter": jnp.clip(jnp.exp(math.log(2.0) - 2.3025851 * jax.random.uniform(seeds[3], (WAVES, F), jnp.float32) ** levels(seeds[3], (WAVES, F), ((0, 8),), -0.2, 0.2)), 0.2, 2.0),
        "mix_pair": scatter_about(seeds[4], (2, F, F), F ** -0.5, 0.5),
        "msg_weight": scatter_about(seeds[5], (F, F), F ** -0.5, 0.5),
        "chan_width": jnp.clip(jnp.exp(jax.random.uniform(seeds[6], (F,), jnp.float32, math.log(1.0), math.log(30.0))), 1.0, 30.0),
        "pair_dist": jnp.clip(1.0 + 24.0 * jax.random.uniform(seeds[7], (ATOMS, NB), jnp.float32) ** levels(seeds[7], (ATOMS, NB), ((0, 512),), -0.2, 0.2), 1.0, 25.0),
        "neighbours": draw_neighbours(jax.random.fold_in(seeds[12], 71), 0),
        "norm_gain": jnp.clip(1.0 + 0.18 * jax.random.normal(seeds[9], (F,), jnp.float32), 0.1, 1.9),
        "in_weight": scatter_about(seeds[10], (F, H), F ** -0.5, 0.5),
        "out_weight": scatter_about(seeds[11], (H, F), H ** -0.5, 0.25),
    }


box_side = 16.0
slab_step = 0.125
two_pi = 2.0 * math.pi

def wave_vectors(wave_index, slab_length):
    counts = wave_index.astype(jnp.float32)
    return jnp.stack([counts[:, 0] * (two_pi / box_side), counts[:, 1] * (two_pi / box_side), counts[:, 2] * (two_pi / slab_length)], axis=0)

def phase_angles(points, wave_vecs):
    return points[:, 0:1] * wave_vecs[0:1, :] + points[:, 1:2] * wave_vecs[1:2, :] + points[:, 2:3] * wave_vecs[2:3, :]

def mix_vectors(s_re, s_im, mix_pair, wave_filter, scale):
    a_re = (s_re * scale).astype(jnp.bfloat16)
    a_im = (s_im * scale).astype(jnp.bfloat16)
    real_real = jnp.dot(a_re, mix_pair[0], preferred_element_type=jnp.float32)
    imag_imag = jnp.dot(a_im, mix_pair[1], preferred_element_type=jnp.float32)
    real_imag = jnp.dot(a_re, mix_pair[1], preferred_element_type=jnp.float32)
    imag_real = jnp.dot(a_im, mix_pair[0], preferred_element_type=jnp.float32)
    y_re = (wave_filter * (real_real - imag_imag)).astype(jnp.bfloat16)
    y_im = (wave_filter * (real_imag + imag_real)).astype(jnp.bfloat16)
    return (y_re, y_im)

def wave_terms(points, wave_vecs, y_re, y_im, inv_scale):
    angles = phase_angles(points, wave_vecs)
    cos_part = jnp.cos(angles).astype(jnp.bfloat16)
    sin_part = jnp.sin(angles).astype(jnp.bfloat16)
    summed = jnp.dot(cos_part, y_re, preferred_element_type=jnp.float32) + jnp.dot(sin_part, y_im, preferred_element_type=jnp.float32)
    return summed * inv_scale

def reference(features, positions, wave_index, wave_filter, mix_pair, msg_weight, chan_width, pair_dist, neighbours, norm_gain, in_weight, out_weight):
    domain = ATOM_DEV * N_KGRP
    halo_width = ATOM_DEV // 4
    projected = jnp.dot(features, msg_weight, preferred_element_type=jnp.float32).astype(jnp.bfloat16)
    row_ids = jnp.arange(ATOMS, dtype=jnp.int32).reshape(N_SPACE, domain)

    def domain_message(block):
        ids, nbr_block, dist_block = block
        local = ids % ATOM_DEV
        source = (ids[:, None] - local[:, None] + nbr_block - halo_width) % ATOMS
        nearby = jnp.take(projected, source.astype(jnp.int32), axis=0)
        weights = jnp.exp(-dist_block[:, :, None] / chan_width[None, None, :])
        return lax.optimization_barrier(jnp.sum(weights * nearby.astype(jnp.float32), axis=1))
    message = lax.map(domain_message, (row_ids, neighbours.reshape(N_SPACE, domain, NB), pair_dist.reshape(N_SPACE, domain, NB))).reshape(ATOMS, F)
    wave_vecs = wave_vectors(wave_index, ATOMS * slab_step)
    feat_blocks = features.reshape(N_SPACE, domain, F)
    pos_blocks = positions.reshape(N_SPACE, domain, 3)
    dims = (((0,), (0,)), ((), ()))

    def add_domain(carry, block):
        feat_block, pos_block = block
        angles = phase_angles(pos_block, wave_vecs)
        cos_part = jnp.cos(angles).astype(jnp.bfloat16)
        sin_part = jnp.sin(angles).astype(jnp.bfloat16)
        new_re = carry[0] + lax.dot_general(cos_part, feat_block, dims, preferred_element_type=jnp.float32)
        new_im = carry[1] + lax.dot_general(sin_part, feat_block, dims, preferred_element_type=jnp.float32)
        return ((new_re, new_im), None)
    zeros = jnp.zeros((WAVES, F), jnp.float32)
    (s_re, s_im), _ = lax.scan(add_domain, (zeros, zeros), (feat_blocks, pos_blocks))
    y_re, y_im = mix_vectors(s_re, s_im, mix_pair, wave_filter, 1.0 / math.sqrt(ATOMS))
    inv_scale = 1.0 / math.sqrt(WAVES)
    ewald = lax.map(lambda pos_block: wave_terms(pos_block, wave_vecs, y_re, y_im, inv_scale), pos_blocks).reshape(ATOMS, F)
    mixed = features.astype(jnp.float32) + message + ewald
    inverse = lax.rsqrt(lax.optimization_barrier(jnp.mean(mixed * mixed, axis=1, keepdims=True)) + 1e-06)
    normed = (mixed * inverse * norm_gain).astype(jnp.bfloat16)
    hidden = jax.nn.silu(jnp.dot(normed, in_weight, preferred_element_type=jnp.float32)).astype(jnp.bfloat16)
    return (mixed + jnp.dot(hidden, out_weight, preferred_element_type=jnp.float32)).astype(jnp.bfloat16)
```

```python
import functools
import math

import jax
import jax.numpy as jnp
import numpy as np
from jax import lax
from jax.experimental import pallas as pl
from jax.experimental.pallas import tpu as pltpu
from jax.sharding import PartitionSpec as P

MESH = pl.DeviceIdType.MESH
BOX = 16.0
SLAB_STEP = 0.125
F = 128
WB = 12
TN = (((0,), (0,)), ((), ()))
NN = (((1,), (0,)), ((), ()))

def fit_poly():
    r = 0.5 * np.cos(np.pi * (np.arange(4001) + 0.5) / 4001 / 2)
    t = r * r
    cheb = np.polynomial.chebyshev
    sin_p = cheb.Chebyshev.fit(t, np.sin(np.pi * r) / r, 4, domain=[0.0, 0.25])
    cos_p = cheb.Chebyshev.fit(t, np.cos(np.pi * r), 5, domain=[0.0, 0.25])
    to = lambda p: tuple(float(v) for v in p.convert(kind=np.polynomial.Polynomial).coef)
    return to(sin_p), to(cos_p)


SIN_C, COS_C = fit_poly()


def cos_sin_turns(u):
    r = u - jnp.round(u)
    t = r * r
    s = jnp.full_like(t, SIN_C[-1])
    for coef in SIN_C[-2::-1]:
        s = s * t + coef
    s = s * r
    c = jnp.full_like(t, COS_C[-1])
    for coef in COS_C[-2::-1]:
        c = c * t + coef
    s2 = s + s
    return 1.0 - s2 * s, s2 * c


def split3(v):
    hi = v.astype(jnp.bfloat16)
    rest = v - hi.astype(jnp.float32)
    mid = rest.astype(jnp.bfloat16)
    low = (rest - mid.astype(jnp.float32)).astype(jnp.bfloat16)
    return hi, mid, low


def low_rows(shape):
    return lax.broadcasted_iota(jnp.int32, shape, len(shape) - 2) < 4


def to_blocks(re, im):
    pairs = re.shape[0] // (2 * WB)
    a = re.reshape(pairs, 3, 8, F)
    b = im.reshape(pairs, 3, 8, F)
    a0, a1, a2 = a[:, 0], a[:, 1], a[:, 2]
    b0, b1, b2 = b[:, 0], b[:, 1], b[:, 2]
    low = low_rows(a1.shape)
    x = jnp.where(low, a1, pltpu.roll(b1, 4, 1))
    y = jnp.where(low, pltpu.roll(a1, 4, 1), b1)
    first = jnp.stack([a0, b0, x], axis=1)
    second = jnp.stack([a2, b2, y], axis=1)
    return jnp.stack([first, second], axis=1).reshape(2 * pairs, 3, 8, F)


def from_blocks(v):
    pairs = v.shape[0] // 2
    v = v.reshape(pairs, 2, 3, 8, F)
    x, y = v[:, 0, 2], v[:, 1, 2]
    low = low_rows(x.shape)
    a1 = jnp.where(low, x, pltpu.roll(y, 4, 1))
    b1 = jnp.where(low, pltpu.roll(x, 4, 1), y)
    re = jnp.stack([v[:, 0, 0], a1, v[:, 1, 0]], axis=1).reshape(pairs * 24, F)
    im = jnp.stack([v[:, 0, 1], b1, v[:, 1, 1]], axis=1).reshape(pairs * 24, F)
    return re, im


def far_first(n):
    return sorted(range(1, n), key=lambda o: -min(o, n - o))


def kernel(
    zs, gs, feat, pos, wave, filt, mix, msgw, width, dist, nbr, gain, inw, outw, out,
    fall, halo, ut, ptc, pts, pc, ps, acc, sc_buf, rc_buf, sy_buf, ry_buf, sz_buf, rz_buf,
    ysrc, yall, yre, yim, es, er, msg_t, own_e,
    ag_s, ag_r, ha_s, ha_r, c_s, c_r, y_s, y_r, z_s, z_r, zb_s, zb_r, yb_s, yb_r, cb_s, cb_r, e_s, e_r,
):
    f32, bf16 = jnp.float32, jnp.bfloat16
    dot = functools.partial(lax.dot_general, preferred_element_type=f32)
    me_s, me_g = lax.axis_index("space"), lax.axis_index("kgrp")
    z, yl, c = me_s // 4, lax.rem(me_s // 2, 2), lax.rem(me_s, 2)
    n_dev = 4 * zs * gs
    flat = me_s * gs + me_g
    up, down = lax.rem(flat + 1, n_dev), lax.rem(flat + n_dev - 1, n_dev)
    up = (up // gs, lax.rem(up, gs))
    down = (down // gs, lax.rem(down, gs))
    group = [(me_s, lax.rem(me_g + o, gs)) for o in range(gs)]
    core = (z * 4 + yl * 2 + 1 - c, me_g)
    ypeer = (z * 4 + (1 - yl) * 2 + c, me_g)
    ring = [(lax.rem(z + o, zs) * 4 + yl * 2 + c, me_g) for o in range(zs)]
    atoms = feat.shape[0]
    kw = wave.shape[1]
    half, quarter = 2 * zs, zs

    def remote(src, dst, send, recv, device):
        return pltpu.make_async_remote_copy(
            src_ref=src, dst_ref=dst, send_sem=send, recv_sem=recv, device_id=device, device_id_type=MESH
        )

    barrier = pltpu.get_barrier_semaphore()
    peers = group[1:] + [up, down, core, ypeer] + ring[1:]
    for device in peers:
        pl.semaphore_signal(barrier, inc=1, device_id=device, device_id_type=MESH)

    scales = lax.broadcasted_iota(jnp.int32, pos.shape, 0)
    scales = jnp.where(scales < 2, 1.0 / BOX, 1.0 / (n_dev * atoms * SLAB_STEP)).astype(f32)
    pieces = split3(pos[...] * scales)
    counts = wave[...].astype(f32).astype(bf16)

    def trig(lhs_rhs, cos_ref, sin_ref):
        total = None
        for lhs, rhs in lhs_rhs:
            part = dot(lhs, rhs, TN)
            total = part if total is None else total + part
        rows, cols = total.shape
        ut[0:rows, 0:cols] = total

        def body(i, carry):
            at = pl.ds(pl.multiple_of(i * 16, 16), 16)
            cos_v, sin_v = cos_sin_turns(ut[at, 0:cols])
            cos_ref[at, :] = cos_v.astype(bf16)
            sin_ref[at, :] = sin_v.astype(bf16)
            return carry

        lax.fori_loop(0, rows // 16, body, 0)

    trig([(counts, p) for p in pieces], ptc, pts)

    pl.semaphore_wait(barrier, len(peers))

    gather = []
    for o in far_first(gs):
        copy = remote(feat, fall.at[me_g], ag_s.at[o], ag_r.at[o], group[o])
        copy.start()
        gather.append((o, copy))
    edge = atoms // 4
    halo_up = remote(feat.at[pl.ds(atoms - edge, edge)], halo.at[0], ha_s.at[0], ha_r.at[0], up)
    halo_down = remote(feat.at[pl.ds(0, edge)], halo.at[1], ha_s.at[1], ha_r.at[1], down)
    halo_up.start()
    halo_down.start()
    fall[pl.ds(me_g, 1)] = feat[...][None]

    for o, copy in gather:
        copy.wait()

    feats = fall[...].reshape(gs * atoms, F)

    def structure(half_index):
        at = pl.ds(pl.multiple_of(half_index * (kw // 2), 8), kw // 2)
        return to_blocks(dot(ptc[at, :], feats, NN), dot(pts[at, :], feats, NN))

    sc_buf[...] = structure(1 - c).astype(bf16)
    copy_c = remote(sc_buf, rc_buf, c_s, c_r, core)
    copy_c.start()
    acc[...] = structure(c)
    copy_c.wait()
    theirs = pl.ds((1 - yl) * quarter, quarter)
    mine = pl.ds(yl * quarter, quarter)
    sy_buf[...] = (acc[theirs] + rc_buf[theirs].astype(f32)).astype(bf16)
    copy_y = remote(sy_buf, ry_buf, y_s, y_r, ypeer)
    copy_y.start()
    acc[mine] = acc[mine] + rc_buf[mine].astype(f32)
    copy_y.wait()
    acc[mine] = acc[mine] + ry_buf[...].astype(f32)
    sz_buf[...] = acc[mine].astype(bf16)
    ring_copies = []
    for o in far_first(zs):
        copy = remote(sz_buf.at[lax.rem(z + o, zs)], rz_buf.at[z], z_s.at[o], z_r.at[o], ring[o])
        copy.start()
        ring_copies.append((o, copy))

    trig([(p, counts) for p in pieces], pc, ps)

    halo_up.wait()
    halo_down.wait()
    weight = msgw[...]
    ext = jnp.concatenate(
        [
            dot(halo[0], weight, NN),
            dot(feat[...], weight, NN),
            dot(halo[1], weight, NN),
            jnp.zeros((edge * 2, F), f32),
        ],
        axis=0,
    )
    ext_t = ext.T.astype(bf16)
    inv_width = (1.0 / jnp.broadcast_to(width[...], (F, F))).T
    row_ids = lax.broadcasted_iota(jnp.int32, (2 * atoms, atoms), 0)
    message = jnp.zeros((F, atoms), f32)
    for j in range(nbr.shape[0]):
        hot = jnp.where(row_ids == nbr[j : j + 1, :], 1.0, 0.0).astype(bf16)
        near = dot(ext_t, hot, NN)
        message = message + jnp.exp(-(dist[j : j + 1, :] * inv_width)) * near
    msg_t[...] = message.T

    own = yl * quarter + z
    total = acc[pl.ds(own, 1)][0]
    for o, copy in ring_copies:
        copy.wait()
        total = total + rz_buf[pl.ds(lax.rem(z + zs - o, zs), 1)][0].astype(f32)

    a = (total * (1.0 / math.sqrt(n_dev * atoms))).reshape(24, F).astype(bf16)
    r0 = dot(a, mix[0], NN).reshape(3, 8, F)
    r1 = dot(a, mix[1], NN).reshape(3, 8, F)
    block = c * half + own
    pair = block // 2
    odd = lax.rem(block, 2) == 1
    fil = filt[pl.ds(pl.multiple_of(pair * 24, 8), 24), :].reshape(3, 8, F)
    low = low_rows((8, F))
    swapped = pltpu.roll(fil[1], 4, 0)
    f_main = jnp.where(odd, fil[2], fil[0])
    f_mixed = jnp.where(jnp.logical_xor(low, odd), fil[1], swapped)
    r1_swapped = pltpu.roll(r1[2], 4, 0)
    y_val = jnp.stack(
        [
            f_main * (r0[0] - r1[1]),
            f_main * (r1[0] + r0[1]),
            f_mixed * jnp.where(low, r0[2] - r1_swapped, r0[2] + r1_swapped),
        ],
        axis=0,
    ).astype(bf16)
    ysrc[...] = y_val
    back = []
    for o in far_first(zs):
        copy = remote(ysrc, yall.at[block], zb_s.at[o], zb_r.at[o], ring[o])
        copy.start()
        back.append(copy)
    yall[pl.ds(block, 1)] = y_val[None]
    for copy in back:
        copy.wait()
    mine_y = yall.at[pl.ds(c * half + yl * quarter, quarter)]
    copy_yb = remote(mine_y, mine_y, yb_s, yb_r, ypeer)
    copy_yb.start()
    copy_yb.wait()
    mine_c = yall.at[pl.ds(c * half, half)]
    copy_cb = remote(mine_c, mine_c, cb_s, cb_r, core)
    copy_cb.start()
    copy_cb.wait()

    re, im = from_blocks(yall[...].astype(f32))
    yre[...] = re.astype(bf16)
    yim[...] = im.astype(bf16)
    inv_scale = 1.0 / math.sqrt(kw * gs)

    def terms(g):
        at = pl.ds(pl.multiple_of(g * atoms, atoms), atoms)
        return (dot(pc[at, :], yre[...], NN) + dot(ps[at, :], yim[...], NN)) * inv_scale

    exchange = []
    for o in far_first(gs):
        es[o] = terms(lax.rem(me_g + o, gs)).astype(bf16)
        copy = remote(es.at[o], er.at[o], e_s.at[o], e_r.at[o], group[o])
        copy.start()
        exchange.append((o, copy))
    ewald = terms(me_g)
    for o, copy in exchange:
        copy.wait()
        ewald = ewald + er[o].astype(f32)

    mixed = feat[...].astype(f32) + msg_t[...] + ewald
    inverse = lax.rsqrt(jnp.mean(mixed * mixed, axis=1, keepdims=True) + 1e-06)
    normed = (mixed * inverse * gain[...]).astype(bf16)
    pre = dot(normed, inw[...], NN)
    hidden = (pre * (1.0 / (1.0 + jnp.exp(-pre)))).astype(bf16)
    out[...] = (mixed + dot(hidden, outw[...], NN)).astype(bf16)


def solution(mesh):
    zs, gs = mesh.shape["space"] // 4, mesh.shape["kgrp"]

    def local(features, positions, wave_index, wave_filter, mix_pair, msg_weight, chan_width, pair_dist,
              neighbours, norm_gain, in_weight, out_weight):
        atoms = features.shape[0]
        dom = gs * atoms
        kw = wave_index.shape[0]
        f32, bf16 = jnp.float32, jnp.bfloat16
        blk = (3, 8, F)
        nb, nh, nq = 4 * zs, 2 * zs, zs
        big = max(kw, dom)
        vm = pltpu.VMEM
        dma = pltpu.SemaphoreType.DMA
        scratch = [
            vm((gs, atoms, F), bf16),
            vm((2, atoms // 4, F), bf16),
            vm((big, big), f32),
            vm((kw, dom), bf16),
            vm((kw, dom), bf16),
            vm((dom, kw), bf16),
            vm((dom, kw), bf16),
            vm((nh, *blk), f32),
            vm((nh, *blk), bf16),
            vm((nh, *blk), bf16),
            vm((nq, *blk), bf16),
            vm((nq, *blk), bf16),
            vm((nq, *blk), bf16),
            vm((nq, *blk), bf16),
            vm(blk, bf16),
            vm((nb, *blk), bf16),
            vm((kw, F), bf16),
            vm((kw, F), bf16),
            vm((gs, atoms, F), bf16),
            vm((gs, atoms, F), bf16),
            vm((atoms, F), f32),
            vm((atoms, F), f32),
            dma((gs,)), dma((gs,)), dma((2,)), dma((2,)),
            dma, dma, dma, dma,
            dma((zs,)), dma((zs,)), dma((zs,)), dma((zs,)),
            dma, dma, dma, dma,
            dma((gs,)), dma((gs,)),
        ]
        return pl.pallas_call(
            functools.partial(kernel, zs, gs),
            out_shape=jax.ShapeDtypeStruct((atoms, F), bf16),
            in_specs=[pl.BlockSpec(memory_space=pltpu.VMEM)] * 12,
            out_specs=pl.BlockSpec(memory_space=pltpu.VMEM),
            scratch_shapes=scratch,
            compiler_params=pltpu.CompilerParams(
                collective_id=0, has_side_effects=True, vmem_limit_bytes=60 * 1024 * 1024
            ),
        )(
            features, positions.T, wave_index.T, wave_filter, mix_pair, msg_weight,
            chan_width.reshape(1, F), pair_dist.T, neighbours.T, norm_gain.reshape(1, F), in_weight, out_weight,
        )

    placed = (
        P(("space", "kgrp"), None), P("space", None), P("kgrp", None), P("kgrp", None), P(), P(), P(),
        P(("space", "kgrp"), None), P(("space", "kgrp"), None), P(), P(), P(),
    )
    return jax.shard_map(
        local, mesh=mesh, in_specs=placed, out_specs=P(("space", "kgrp"), None), check_vma=False
    )
```

```python
import functools
import math

import jax
import jax.numpy as jnp
import numpy as np
from jax import lax
from jax.experimental import pallas as pl
from jax.experimental.pallas import tpu as pltpu
from jax.sharding import PartitionSpec as P

MESH = pl.DeviceIdType.MESH
BOX = 16.0
SLAB_STEP = 0.125
F = 128
WB = 12
TN = (((0,), (0,)), ((), ()))
NN = (((1,), (0,)), ((), ()))

def fit_poly():
    r = 0.5 * np.cos(np.pi * (np.arange(4001) + 0.5) / 4001 / 2)
    t = r * r
    cheb = np.polynomial.chebyshev
    sin_p = cheb.Chebyshev.fit(t, np.sin(np.pi * r) / r, 4, domain=[0.0, 0.25])
    cos_p = cheb.Chebyshev.fit(t, np.cos(np.pi * r), 5, domain=[0.0, 0.25])
    to = lambda p: tuple(float(v) for v in p.convert(kind=np.polynomial.Polynomial).coef)
    return to(sin_p), to(cos_p)


SIN_C, COS_C = fit_poly()


def cos_sin_turns(u):
    r = u - jnp.round(u)
    t = r * r
    s = jnp.full_like(t, SIN_C[-1])
    for coef in SIN_C[-2::-1]:
        s = s * t + coef
    s = s * r
    c = jnp.full_like(t, COS_C[-1])
    for coef in COS_C[-2::-1]:
        c = c * t + coef
    s2 = s + s
    return 1.0 - s2 * s, s2 * c


def split3(v):
    hi = v.astype(jnp.bfloat16)
    rest = v - hi.astype(jnp.float32)
    mid = rest.astype(jnp.bfloat16)
    low = (rest - mid.astype(jnp.float32)).astype(jnp.bfloat16)
    return hi, mid, low


def low_rows(shape):
    return lax.broadcasted_iota(jnp.int32, shape, len(shape) - 2) < 4


def to_blocks(re, im):
    pairs = re.shape[0] // (2 * WB)
    a = re.reshape(pairs, 3, 8, F)
    b = im.reshape(pairs, 3, 8, F)
    a0, a1, a2 = a[:, 0], a[:, 1], a[:, 2]
    b0, b1, b2 = b[:, 0], b[:, 1], b[:, 2]
    low = low_rows(a1.shape)
    x = jnp.where(low, a1, pltpu.roll(b1, 4, 1))
    y = jnp.where(low, pltpu.roll(a1, 4, 1), b1)
    first = jnp.stack([a0, b0, x], axis=1)
    second = jnp.stack([a2, b2, y], axis=1)
    return jnp.stack([first, second], axis=1).reshape(2 * pairs, 3, 8, F)


def from_blocks(v):
    pairs = v.shape[0] // 2
    v = v.reshape(pairs, 2, 3, 8, F)
    x, y = v[:, 0, 2], v[:, 1, 2]
    low = low_rows(x.shape)
    a1 = jnp.where(low, x, pltpu.roll(y, 4, 1))
    b1 = jnp.where(low, pltpu.roll(x, 4, 1), y)
    re = jnp.stack([v[:, 0, 0], a1, v[:, 1, 0]], axis=1).reshape(pairs * 24, F)
    im = jnp.stack([v[:, 0, 1], b1, v[:, 1, 1]], axis=1).reshape(pairs * 24, F)
    return re, im


def far_first(n):
    return sorted(range(1, n), key=lambda o: -min(o, n - o))


def slot_of(o, n):
    return 0 if o == 0 else 2 * o - 1 if o <= n // 2 else 2 * (n - o)


def kernel(
    zs, gs, feat, pos, wave, filt, mix, msgw, width, dist, nbr, gain, inw, outw, out,
    fall, halo, ut, ptc, pts, pc, ps, stage, acc, sc_buf, rc_buf, sy_buf, ry_buf, sz_buf, rz_buf,
    ysrc, yall, yre, yim, es, er, msg_t,
    know, ag_s, ag_r, ha_s, ha_r, c_s, c_r, y_s, y_r, z_s, z_r, zb_s, zb_r, yb_s, yb_r, cb_s, cb_r, e_s, e_r,
):
    f32, bf16 = jnp.float32, jnp.bfloat16
    dot = functools.partial(lax.dot_general, preferred_element_type=f32)
    me_s, me_g = lax.axis_index("space"), lax.axis_index("kgrp")
    z, yl, c = me_s // 4, lax.rem(me_s // 2, 2), lax.rem(me_s, 2)
    n_dev = 4 * zs * gs
    flat = me_s * gs + me_g
    up, down = lax.rem(flat + 1, n_dev), lax.rem(flat + n_dev - 1, n_dev)
    up = (up // gs, lax.rem(up, gs))
    down = (down // gs, lax.rem(down, gs))
    group = [(me_s, lax.rem(me_g + o, gs)) for o in range(gs)]
    core = (z * 4 + yl * 2 + 1 - c, me_g)
    ypeer = (z * 4 + (1 - yl) * 2 + c, me_g)
    ring_z = [lax.rem(z + o, zs) for o in range(zs)]
    ring = [(at * 4 + yl * 2 + c, me_g) for at in ring_z]
    offset_of = sorted(range(zs), key=lambda o: slot_of(o, zs))
    atoms = feat.shape[0]
    kw = wave.shape[1]
    rows = kw // 4

    def remote(src, dst, send, recv, device):
        return pltpu.make_async_remote_copy(
            src_ref=src, dst_ref=dst, send_sem=send, recv_sem=recv, device_id=device, device_id_type=MESH
        )

    def signal(sem, device):
        pl.semaphore_signal(sem, inc=1, device_id=device, device_id_type=MESH)

    barrier = pltpu.get_barrier_semaphore()
    peers = group[1:] + [up, down, core, ypeer, ring[1], ring[zs - 1]]
    for device in peers:
        signal(barrier, device)

    scales = lax.broadcasted_iota(jnp.int32, pos.shape, 0)
    scales = jnp.where(scales < 2, 1.0 / BOX, 1.0 / (n_dev * atoms * SLAB_STEP)).astype(f32)
    pieces = split3(pos[...] * scales)
    counts = wave[...].astype(f32).astype(bf16)

    pl.semaphore_wait(barrier, len(peers))

    gather = []
    for o in far_first(gs):
        copy = remote(feat, fall.at[me_g], ag_s.at[o], ag_r.at[o], group[o])
        copy.start()
        gather.append(copy)
    edge = atoms // 4
    halo_up = remote(feat.at[pl.ds(atoms - edge, edge)], halo.at[0], ha_s.at[0], ha_r.at[0], up)
    halo_down = remote(feat.at[pl.ds(0, edge)], halo.at[1], ha_s.at[1], ha_r.at[1], down)
    halo_up.start()
    halo_down.start()
    fall[pl.ds(me_g, 1)] = feat[...][None]

    steps = []
    reach = 1
    while reach < zs // 2:
        steps.append(reach)
        reach *= 2

    def tell(i):
        if i < len(steps):
            signal(know.at[i], ring[steps[i]])
            signal(know.at[i], ring[zs - steps[i]])

    def hear(i):
        if i < len(steps):
            pl.semaphore_wait(know.at[i], 2)

    tell(0)

    def trig(lhs_rhs, cos_ref, sin_ref):
        total = None
        for lhs, rhs in lhs_rhs:
            part = dot(lhs, rhs, TN)
            total = part if total is None else total + part
        n, cols = total.shape
        ut[0:n, 0:cols] = total

        def body(i, carry):
            at = pl.ds(pl.multiple_of(i * 16, 16), 16)
            cos_v, sin_v = cos_sin_turns(ut[at, 0:cols])
            cos_ref[at, :] = cos_v.astype(bf16)
            sin_ref[at, :] = sin_v.astype(bf16)
            return carry

        lax.fori_loop(0, n // 16, body, 0)

    trig([(counts, p) for p in pieces], ptc, pts)
    hear(0)
    tell(1)

    for copy in gather:
        copy.wait()
    hear(1)
    tell(2)

    feats = fall[...].reshape(gs * atoms, F)

    def structure(core_at, y_at):
        at = pl.ds(pl.multiple_of((core_at * 2 + y_at) * rows, 8), rows)
        stage[...] = to_blocks(dot(ptc[at, :], feats, NN), dot(pts[at, :], feats, NN))
        return [stage[pl.ds(ring_z[o], 1)][0] for o in offset_of]

    core_copies = []
    for i, y_at in enumerate((1 - yl, yl)):
        for s, v in enumerate(structure(1 - c, y_at)):
            sc_buf[i, s] = v.astype(bf16)
        copy = remote(sc_buf.at[i], rc_buf.at[i], c_s.at[i], c_r.at[i], core)
        copy.start()
        core_copies.append(copy)
    cut = zs // 2
    parts = (pl.ds(cut, zs - cut), pl.ds(0, cut))
    mine = structure(c, 1 - yl)
    core_copies[0].wait()
    y_copies = []
    for i, (lo, hi) in enumerate(((cut, zs), (0, cut))):
        for s in range(lo, hi):
            sy_buf[s] = (mine[s] + rc_buf[0, s].astype(f32)).astype(bf16)
        copy = remote(sy_buf.at[parts[i]], ry_buf.at[parts[i]], y_s.at[i], y_r.at[i], ypeer)
        copy.start()
        y_copies.append(copy)
    mine = structure(c, yl)
    core_copies[1].wait()
    for s in range(zs):
        acc[s] = mine[s] + rc_buf[1, s].astype(f32)
    hear(2)
    ring_copies = []
    for i, (lo, hi) in enumerate(((cut, zs), (0, cut))):
        y_copies[i].wait()
        for s in range(hi - 1, lo - 1, -1):
            total = acc[s] + ry_buf[s].astype(f32)
            if s == 0:
                acc[0] = total
                continue
            sz_buf[s] = total.astype(bf16)
            o = offset_of[s]
            back_slot = slot_of(zs - o, zs)
            copy = remote(sz_buf.at[s], rz_buf.at[back_slot], z_s.at[s], z_r.at[back_slot], ring[o])
            copy.start()
            ring_copies.append(copy)

    trig([(p, counts) for p in pieces], pc, ps)

    total = acc[0]
    for copy in ring_copies:
        copy.wait()
    for s in range(1, zs):
        total = total + rz_buf[s].astype(f32)

    a = (total * (1.0 / math.sqrt(n_dev * atoms))).reshape(24, F).astype(bf16)
    r0 = dot(a, mix[0], NN).reshape(3, 8, F)
    r1 = dot(a, mix[1], NN).reshape(3, 8, F)
    odd = lax.rem(z, 2) == 1
    pair = ((c * 2 + yl) * zs + z) // 2
    fil = filt[pl.ds(pl.multiple_of(pair * 24, 8), 24), :].reshape(3, 8, F)
    low = low_rows((8, F))
    swapped = pltpu.roll(fil[1], 4, 0)
    f_main = jnp.where(odd, fil[2], fil[0])
    f_mixed = jnp.where(jnp.logical_xor(low, odd), fil[1], swapped)
    r1_swapped = pltpu.roll(r1[2], 4, 0)
    y_val = jnp.stack(
        [
            f_main * (r0[0] - r1[1]),
            f_main * (r1[0] + r0[1]),
            f_mixed * jnp.where(low, r0[2] - r1_swapped, r0[2] + r1_swapped),
        ],
        axis=0,
    ).astype(bf16)
    ysrc[...] = y_val
    here = c * 2 + yl
    beside = c * 2 + 1 - yl
    back = {}
    for o in far_first(zs):
        s = slot_of(zs - o, zs)
        copy = remote(ysrc, yall.at[here, s], zb_s.at[s], zb_r.at[s], ring[o])
        copy.start()
        back[s] = copy
    yall[pl.ds(here, 1), 0] = y_val[None]

    halo_up.wait()
    halo_down.wait()
    weight = msgw[...]
    ext = jnp.concatenate(
        [
            dot(halo[0], weight, NN),
            dot(feat[...], weight, NN),
            dot(halo[1], weight, NN),
            jnp.zeros((edge * 2, F), f32),
        ],
        axis=0,
    )
    ext_t = ext.T.astype(bf16)
    inv_width = (1.0 / jnp.broadcast_to(width[...], (F, F))).T
    row_ids = lax.broadcasted_iota(jnp.int32, (2 * atoms, atoms), 0)
    message = jnp.zeros((F, atoms), f32)
    for j in range(nbr.shape[0]):
        hot = jnp.where(row_ids == nbr[j : j + 1, :], 1.0, 0.0).astype(bf16)
        near = dot(ext_t, hot, NN)
        message = message + jnp.exp(-(dist[j : j + 1, :] * inv_width)) * near
    msg_t[...] = message.T

    if zs == 16:
        cuts = (0, 5, 9, 13, 16)
    else:
        cuts = (0, zs // 2, zs)
    y_back, core_back = [], []
    for i in range(len(cuts) - 1):
        lo, hi = cuts[i], cuts[i + 1]
        for s in range(max(lo, 1), hi):
            back[s].wait()
        here_part = yall.at[here, pl.ds(lo, hi - lo)]
        copy = remote(here_part, here_part, yb_s.at[i], yb_r.at[i], ypeer)
        copy.start()
        y_back.append(copy)
        copy = remote(here_part, here_part, cb_s.at[i], cb_r.at[i], core)
        copy.start()
        core_back.append(copy)
        beside_part = yall.at[beside, pl.ds(lo, hi - lo)]
        copy = remote(beside_part, beside_part, cb_s.at[4 + i], cb_r.at[4 + i], core)
        core_back.append(copy)
        if i > 0:
            y_back[i - 1].wait()
            core_back[2 * i - 1].start()
    y_back[-1].wait()
    core_back[-1].start()
    for copy in core_back:
        copy.wait()

    slots = []
    for t in range(zs):
        o = lax.rem(t - z + zs, zs)
        slots.append(jnp.where(o <= zs // 2, jnp.maximum(2 * o - 1, 0), 2 * (zs - o)))
    for q in range(4):
        blocks = [yall[q, pl.ds(slots[t], 1)] for t in range(zs)]
        re, im = from_blocks(jnp.concatenate(blocks, axis=0).astype(f32))
        yre[q * rows : (q + 1) * rows, :] = re.astype(bf16)
        yim[q * rows : (q + 1) * rows, :] = im.astype(bf16)
    inv_scale = 1.0 / math.sqrt(kw * gs)

    def terms(g):
        at = pl.ds(pl.multiple_of(g * atoms, atoms), atoms)
        return (dot(pc[at, :], yre[...], NN) + dot(ps[at, :], yim[...], NN)) * inv_scale

    exchange = []
    for o in far_first(gs):
        es[o] = terms(lax.rem(me_g + o, gs)).astype(bf16)
        copy = remote(es.at[o], er.at[o], e_s.at[o], e_r.at[o], group[o])
        copy.start()
        exchange.append((o, copy))
    ewald = terms(me_g)
    for o, copy in exchange:
        copy.wait()
        ewald = ewald + er[o].astype(f32)

    mixed = feat[...].astype(f32) + msg_t[...] + ewald
    inverse = lax.rsqrt(jnp.mean(mixed * mixed, axis=1, keepdims=True) + 1e-06)
    normed = (mixed * inverse * gain[...]).astype(bf16)
    pre = dot(normed, inw[...], NN)
    hidden = (pre * (1.0 / (1.0 + jnp.exp(-pre)))).astype(bf16)
    out[...] = (mixed + dot(hidden, outw[...], NN)).astype(bf16)


def solution(mesh):
    zs, gs = mesh.shape["space"] // 4, mesh.shape["kgrp"]

    def local(features, positions, wave_index, wave_filter, mix_pair, msg_weight, chan_width, pair_dist,
              neighbours, norm_gain, in_weight, out_weight):
        atoms = features.shape[0]
        dom = gs * atoms
        kw = wave_index.shape[0]
        f32, bf16 = jnp.float32, jnp.bfloat16
        blk = (3, 8, F)
        big = max(kw, dom)
        vm = pltpu.VMEM
        dma = pltpu.SemaphoreType.DMA
        scratch = [
            vm((gs, atoms, F), bf16),
            vm((2, atoms // 4, F), bf16),
            vm((big, big), f32),
            vm((kw, dom), bf16),
            vm((kw, dom), bf16),
            vm((dom, kw), bf16),
            vm((dom, kw), bf16),
            vm((zs, *blk), f32),
            vm((zs, *blk), f32),
            vm((2, zs, *blk), bf16),
            vm((2, zs, *blk), bf16),
            vm((zs, *blk), bf16),
            vm((zs, *blk), bf16),
            vm((zs, *blk), bf16),
            vm((zs, *blk), bf16),
            vm(blk, bf16),
            vm((4, zs, *blk), bf16),
            vm((kw, F), bf16),
            vm((kw, F), bf16),
            vm((gs, atoms, F), bf16),
            vm((gs, atoms, F), bf16),
            vm((atoms, F), f32),
            pltpu.SemaphoreType.REGULAR((4,)),
            dma((gs,)), dma((gs,)), dma((2,)), dma((2,)),
            dma((2,)), dma((2,)), dma((2,)), dma((2,)),
            dma((zs,)), dma((zs,)), dma((zs,)), dma((zs,)),
            dma((4,)), dma((4,)), dma((8,)), dma((8,)),
            dma((gs,)), dma((gs,)),
        ]
        return pl.pallas_call(
            functools.partial(kernel, zs, gs),
            out_shape=jax.ShapeDtypeStruct((atoms, F), bf16),
            in_specs=[pl.BlockSpec(memory_space=pltpu.VMEM)] * 12,
            out_specs=pl.BlockSpec(memory_space=pltpu.VMEM),
            scratch_shapes=scratch,
            compiler_params=pltpu.CompilerParams(
                collective_id=0, has_side_effects=True, vmem_limit_bytes=60 * 1024 * 1024
            ),
        )(
            features, positions.T, wave_index.T, wave_filter, mix_pair, msg_weight,
            chan_width.reshape(1, F), pair_dist.T, neighbours.T, norm_gain.reshape(1, F), in_weight, out_weight,
        )

    placed = (
        P(("space", "kgrp"), None), P("space", None), P("kgrp", None), P("kgrp", None), P(), P(), P(),
        P(("space", "kgrp"), None), P(("space", "kgrp"), None), P(), P(), P(),
    )
    return jax.shard_map(
        local, mesh=mesh, in_specs=placed, out_specs=P(("space", "kgrp"), None), check_vma=False
    )
```

```python
import functools
import math

import jax
import jax.numpy as jnp
import numpy as np
from jax import lax
from jax.experimental import pallas as pl
from jax.experimental.pallas import tpu as pltpu
from jax.sharding import PartitionSpec as P

MESH = pl.DeviceIdType.MESH
BOX = 16.0
SLAB_STEP = 0.125
F = 128
WB = 12
TN = (((0,), (0,)), ((), ()))
NN = (((1,), (0,)), ((), ()))

def fit_poly():
    r = 0.5 * np.cos(np.pi * (np.arange(4001) + 0.5) / 4001 / 2)
    t = r * r
    cheb = np.polynomial.chebyshev
    sin_p = cheb.Chebyshev.fit(t, np.sin(np.pi * r) / r, 4, domain=[0.0, 0.25])
    cos_p = cheb.Chebyshev.fit(t, np.cos(np.pi * r), 5, domain=[0.0, 0.25])
    to = lambda p: tuple(float(v) for v in p.convert(kind=np.polynomial.Polynomial).coef)
    return to(sin_p), to(cos_p)


SIN_C, COS_C = fit_poly()


def cos_sin_turns(u):
    r = u - jnp.round(u)
    t = r * r
    s = jnp.full_like(t, SIN_C[-1])
    for coef in SIN_C[-2::-1]:
        s = s * t + coef
    s = s * r
    c = jnp.full_like(t, COS_C[-1])
    for coef in COS_C[-2::-1]:
        c = c * t + coef
    s2 = s + s
    return 1.0 - s2 * s, s2 * c


def split3(v):
    hi = v.astype(jnp.bfloat16)
    rest = v - hi.astype(jnp.float32)
    mid = rest.astype(jnp.bfloat16)
    low = (rest - mid.astype(jnp.float32)).astype(jnp.bfloat16)
    return hi, mid, low


def low_rows(shape):
    return lax.broadcasted_iota(jnp.int32, shape, len(shape) - 2) < 4


def to_blocks(re, im):
    pairs = re.shape[0] // (2 * WB)
    a = re.reshape(pairs, 3, 8, F)
    b = im.reshape(pairs, 3, 8, F)
    a0, a1, a2 = a[:, 0], a[:, 1], a[:, 2]
    b0, b1, b2 = b[:, 0], b[:, 1], b[:, 2]
    low = low_rows(a1.shape)
    x = jnp.where(low, a1, pltpu.roll(b1, 4, 1))
    y = jnp.where(low, pltpu.roll(a1, 4, 1), b1)
    first = jnp.stack([a0, b0, x], axis=1)
    second = jnp.stack([a2, b2, y], axis=1)
    return jnp.stack([first, second], axis=1).reshape(2 * pairs, 3, 8, F)


def from_blocks(v):
    pairs = v.shape[0] // 2
    v = v.reshape(pairs, 2, 3, 8, F)
    x, y = v[:, 0, 2], v[:, 1, 2]
    low = low_rows(x.shape)
    a1 = jnp.where(low, x, pltpu.roll(y, 4, 1))
    b1 = jnp.where(low, pltpu.roll(x, 4, 1), y)
    re = jnp.stack([v[:, 0, 0], a1, v[:, 1, 0]], axis=1).reshape(pairs * 24, F)
    im = jnp.stack([v[:, 0, 1], b1, v[:, 1, 1]], axis=1).reshape(pairs * 24, F)
    return re, im


def far_first(n):
    return sorted(range(1, n), key=lambda o: -min(o, n - o))


def slot_of(o, n):
    return 0 if o == 0 else 2 * o - 1 if o <= n // 2 else 2 * (n - o)


def kernel(
    zs, gs, feat, pos, wave, filt, mix, msgw, width, dist, nbr, gain, inw, outw, out,
    fall, halo, ut, ptc, pts, pc, ps, stage, acc, sc_buf, rc_buf, sy_buf, ry_buf, sz_buf, rz_buf,
    ysrc, yall, yre, yim, es, er, msg_t, fil_v, mix_v, inw_v, outw_v,
    know, in_s, ag_s, ag_r, ha_s, ha_r, c_s, c_r, y_s, y_r, z_s, z_r, zb_s, zb_r, yb_s, yb_r, cb_s, cb_r, e_s, e_r,
):
    f32, bf16 = jnp.float32, jnp.bfloat16
    dot = functools.partial(lax.dot_general, preferred_element_type=f32)
    me_s, me_g = lax.axis_index("space"), lax.axis_index("kgrp")
    z, yl, c = me_s // 4, lax.rem(me_s // 2, 2), lax.rem(me_s, 2)
    n_dev = 4 * zs * gs
    flat = me_s * gs + me_g
    up, down = lax.rem(flat + 1, n_dev), lax.rem(flat + n_dev - 1, n_dev)
    up = (up // gs, lax.rem(up, gs))
    down = (down // gs, lax.rem(down, gs))
    group = [(me_s, lax.rem(me_g + o, gs)) for o in range(gs)]
    core = (z * 4 + yl * 2 + 1 - c, me_g)
    ypeer = (z * 4 + (1 - yl) * 2 + c, me_g)
    ring_z = [lax.rem(z + o, zs) for o in range(zs)]
    ring = [(at * 4 + yl * 2 + c, me_g) for at in ring_z]
    offset_of = sorted(range(zs), key=lambda o: slot_of(o, zs))
    atoms = feat.shape[0]
    kw = wave.shape[1]
    rows = kw // 4

    def remote(src, dst, send, recv, device):
        return pltpu.make_async_remote_copy(
            src_ref=src, dst_ref=dst, send_sem=send, recv_sem=recv, device_id=device, device_id_type=MESH
        )

    def signal(sem, device):
        pl.semaphore_signal(sem, inc=1, device_id=device, device_id_type=MESH)

    barrier = pltpu.get_barrier_semaphore()
    peers = group[1:] + [up, down, core, ypeer, ring[1], ring[zs - 1]]
    for device in peers:
        signal(barrier, device)

    pair = ((c * 2 + yl) * zs + z) // 2
    fetch = [
        pltpu.make_async_copy(src, dst, in_s.at[i])
        for i, (src, dst) in enumerate(
            ((filt.at[pl.ds(pl.multiple_of(pair * 24, 8), 24)], fil_v), (mix, mix_v), (inw, inw_v), (outw, outw_v))
        )
    ]
    for copy in fetch:
        copy.start()

    turned = [pos[:, pl.ds(pl.multiple_of(at * atoms, atoms), atoms)] for _, at in group]
    scales = lax.broadcasted_iota(jnp.int32, pos.shape, 0)
    scales = jnp.where(scales < 2, 1.0 / BOX, 1.0 / (n_dev * atoms * SLAB_STEP)).astype(f32)
    pieces = split3(jnp.concatenate(turned, axis=1) * scales)
    counts = wave[...].astype(f32).astype(bf16)

    pl.semaphore_wait(barrier, len(peers))

    for o in far_first(gs):
        remote(feat, fall.at[gs - o], ag_s, ag_r, group[o]).start()
    edge = atoms // 4
    remote(feat.at[pl.ds(atoms - edge, edge)], halo.at[0], ha_s, ha_r, up).start()
    remote(feat.at[pl.ds(0, edge)], halo.at[1], ha_s, ha_r, down).start()
    fall[0] = feat[...]

    def received(ref, sem):
        remote(ref, ref, ag_s, sem, core).wait_recv()

    def sent(ref, sem):
        remote(ref, ref, sem, ag_r, core).wait_send()

    steps = []
    reach = 1
    while reach < zs // 2:
        steps.append(reach)
        reach *= 2

    def tell(i):
        if i < len(steps):
            signal(know.at[i], ring[steps[i]])
            signal(know.at[i], ring[zs - steps[i]])

    def hear(i):
        if i < len(steps):
            pl.semaphore_wait(know.at[i], 2)

    tell(0)

    def trig(lhs_rhs, cos_ref, sin_ref):
        total = None
        for lhs, rhs in lhs_rhs:
            part = dot(lhs, rhs, TN)
            total = part if total is None else total + part
        n, cols = total.shape
        ut[0:n, 0:cols] = total

        def body(i, carry):
            at = pl.ds(pl.multiple_of(i * 16, 16), 16)
            cos_v, sin_v = cos_sin_turns(ut[at, 0:cols])
            cos_ref[at, :] = cos_v.astype(bf16)
            sin_ref[at, :] = sin_v.astype(bf16)
            return carry

        lax.fori_loop(0, n // 16, body, 0)

    trig([(counts, p) for p in pieces], ptc, pts)
    hear(0)
    tell(1)
    trig([(p, counts) for p in pieces], pc, ps)
    hear(1)
    tell(2)
    if gs > 1:
        received(fall.at[pl.ds(1, gs - 1)], ag_r)

    feats = fall[...].reshape(gs * atoms, F)

    def structure(core_at, y_at):
        at = pl.ds(pl.multiple_of((core_at * 2 + y_at) * rows, 8), rows)
        stage[...] = to_blocks(dot(ptc[at, :], feats, NN), dot(pts[at, :], feats, NN))
        return [stage[pl.ds(ring_z[o], 1)][0] for o in offset_of]

    for i, y_at in enumerate((1 - yl, yl)):
        for s, v in enumerate(structure(1 - c, y_at)):
            sc_buf[i, s] = v.astype(bf16)
        remote(sc_buf.at[i], rc_buf.at[i], c_s, c_r.at[i], core).start()
    cut = zs // 2
    parts = ((cut, zs), (0, cut))
    mine = structure(c, 1 - yl)
    received(rc_buf.at[0], c_r.at[0])
    for i, (lo, hi) in enumerate(parts):
        for s in range(lo, hi):
            sy_buf[s] = (mine[s] + rc_buf[0, s].astype(f32)).astype(bf16)
        part = pl.ds(lo, hi - lo)
        remote(sy_buf.at[part], ry_buf.at[part], y_s, y_r.at[i], ypeer).start()
    mine = structure(c, yl)
    received(rc_buf.at[1], c_r.at[1])
    for s in range(zs):
        acc[s] = mine[s] + rc_buf[1, s].astype(f32)
    hear(2)
    for i, (lo, hi) in enumerate(parts):
        received(ry_buf.at[pl.ds(lo, hi - lo)], y_r.at[i])
        for s in range(hi - 1, lo - 1, -1):
            total = acc[s] + ry_buf[s].astype(f32)
            if s == 0:
                acc[0] = total
                continue
            sz_buf[s] = total.astype(bf16)
            o = offset_of[s]
            remote(sz_buf.at[s], rz_buf.at[slot_of(zs - o, zs)], z_s, z_r, ring[o]).start()

    for copy in fetch:
        copy.wait()
    total = acc[0]
    others = pl.ds(1, zs - 1)
    received(rz_buf.at[others], z_r)
    for s in range(1, zs):
        total = total + rz_buf[s].astype(f32)

    a = (total * (1.0 / math.sqrt(n_dev * atoms))).reshape(24, F).astype(bf16)
    r0 = dot(a, mix_v[0], NN).reshape(3, 8, F)
    r1 = dot(a, mix_v[1], NN).reshape(3, 8, F)
    odd = lax.rem(z, 2) == 1
    fil = fil_v[...].reshape(3, 8, F)
    low = low_rows((8, F))
    swapped = pltpu.roll(fil[1], 4, 0)
    f_main = jnp.where(odd, fil[2], fil[0])
    f_mixed = jnp.where(jnp.logical_xor(low, odd), fil[1], swapped)
    r1_swapped = pltpu.roll(r1[2], 4, 0)
    y_val = jnp.stack(
        [
            f_main * (r0[0] - r1[1]),
            f_main * (r1[0] + r0[1]),
            f_mixed * jnp.where(low, r0[2] - r1_swapped, r0[2] + r1_swapped),
        ],
        axis=0,
    ).astype(bf16)
    ysrc[...] = y_val
    here = c * 2 + yl
    beside = c * 2 + 1 - yl
    cuts = (0, 5, 9, 13, 16) if zs == 16 else (0, zs // 2, zs)
    for o in far_first(zs):
        s = slot_of(zs - o, zs)
        part = sum(s >= hi for hi in cuts[1:])
        remote(ysrc, yall.at[here, s], zb_s, zb_r.at[part], ring[o]).start()
    yall[pl.ds(here, 1), 0] = y_val[None]

    received(halo, ha_r)
    weight = msgw[...]
    ext = jnp.concatenate(
        [
            dot(halo[0], weight, NN),
            dot(feat[...], weight, NN),
            dot(halo[1], weight, NN),
            jnp.zeros((edge * 2, F), f32),
        ],
        axis=0,
    )
    ext_t = ext.T.astype(bf16)
    inv_width = (1.0 / jnp.broadcast_to(width[...], (F, F))).T
    row_ids = lax.broadcasted_iota(jnp.int32, (2 * atoms, atoms), 0)
    message = jnp.zeros((F, atoms), f32)
    for j in range(nbr.shape[0]):
        hot = jnp.where(row_ids == nbr[j : j + 1, :], 1.0, 0.0).astype(bf16)
        near = dot(ext_t, hot, NN)
        message = message + jnp.exp(-(dist[j : j + 1, :] * inv_width)) * near
    msg_t[...] = message.T

    for i in range(len(cuts) - 1):
        lo, hi = cuts[i], cuts[i + 1]
        if hi > max(lo, 1):
            received(yall.at[here, pl.ds(max(lo, 1), hi - max(lo, 1))], zb_r.at[i])
        here_part = yall.at[here, pl.ds(lo, hi - lo)]
        remote(here_part, here_part, yb_s, yb_r.at[i], ypeer).start()
        remote(here_part, here_part, cb_s, cb_r, core).start()
    for i in range(len(cuts) - 1):
        beside_part = yall.at[beside, pl.ds(cuts[i], cuts[i + 1] - cuts[i])]
        received(beside_part, yb_r.at[i])
        remote(beside_part, beside_part, cb_s, cb_r, core).start()
    received(yall.at[pl.ds((1 - c) * 2, 2)], cb_r)

    slots = []
    for t in range(zs):
        o = lax.rem(t - z + zs, zs)
        slots.append(jnp.where(o <= zs // 2, jnp.maximum(2 * o - 1, 0), 2 * (zs - o)))
    for q in range(4):
        blocks = [yall[q, pl.ds(slots[t], 1)] for t in range(zs)]
        re, im = from_blocks(jnp.concatenate(blocks, axis=0).astype(f32))
        yre[q * rows : (q + 1) * rows, :] = re.astype(bf16)
        yim[q * rows : (q + 1) * rows, :] = im.astype(bf16)
    inv_scale = 1.0 / math.sqrt(kw * gs)

    def terms(o):
        at = slice(o * atoms, (o + 1) * atoms)
        return (dot(pc[at, :], yre[...], NN) + dot(ps[at, :], yim[...], NN)) * inv_scale

    for o in far_first(gs):
        es[o] = terms(o).astype(bf16)
        remote(es.at[o], er.at[gs - o], e_s, e_r, group[o]).start()
    ewald = terms(0)

    sent(halo, ha_s)
    sent(sc_buf, c_s)
    sent(sy_buf, y_s)
    sent(sz_buf.at[others], z_s)
    sent(yall.at[here, others], zb_s)
    sent(yall.at[here], yb_s)
    sent(yall.at[pl.ds(c * 2, 2)], cb_s)
    if gs > 1:
        rest = pl.ds(1, gs - 1)
        sent(fall.at[rest], ag_s)
        received(er.at[rest], e_r)
        sent(es.at[rest], e_s)
    for o in range(1, gs):
        ewald = ewald + er[o].astype(f32)

    mixed = feat[...].astype(f32) + msg_t[...] + ewald
    inverse = lax.rsqrt(jnp.mean(mixed * mixed, axis=1, keepdims=True) + 1e-06)
    normed = (mixed * inverse * gain[...]).astype(bf16)
    pre = dot(normed, inw_v[...], NN)
    hidden = (pre * (1.0 / (1.0 + jnp.exp(-pre)))).astype(bf16)
    out[...] = (mixed + dot(hidden, outw_v[...], NN)).astype(bf16)


def solution(mesh):
    zs, gs = mesh.shape["space"] // 4, mesh.shape["kgrp"]

    def local(features, positions, wave_index, wave_filter, mix_pair, msg_weight, chan_width, pair_dist,
              neighbours, norm_gain, in_weight, out_weight):
        atoms = features.shape[0]
        dom = gs * atoms
        kw = wave_index.shape[0]
        f32, bf16 = jnp.float32, jnp.bfloat16
        blk = (3, 8, F)
        big = max(kw, dom)
        vm = pltpu.VMEM
        any_, vmem = pl.BlockSpec(memory_space=pl.ANY), pl.BlockSpec(memory_space=pltpu.VMEM)
        dma = pltpu.SemaphoreType.DMA
        scratch = [
            vm((gs, atoms, F), bf16),
            vm((2, atoms // 4, F), bf16),
            vm((big, big), f32),
            vm((kw, dom), bf16),
            vm((kw, dom), bf16),
            vm((dom, kw), bf16),
            vm((dom, kw), bf16),
            vm((zs, *blk), f32),
            vm((zs, *blk), f32),
            vm((2, zs, *blk), bf16),
            vm((2, zs, *blk), bf16),
            vm((zs, *blk), bf16),
            vm((zs, *blk), bf16),
            vm((zs, *blk), bf16),
            vm((zs, *blk), bf16),
            vm(blk, bf16),
            vm((4, zs, *blk), bf16),
            vm((kw, F), bf16),
            vm((kw, F), bf16),
            vm((gs, atoms, F), bf16),
            vm((gs, atoms, F), bf16),
            vm((atoms, F), f32),
            vm((2 * WB, F), f32),
            vm(mix_pair.shape, bf16),
            vm(in_weight.shape, bf16),
            vm(out_weight.shape, bf16),
            pltpu.SemaphoreType.REGULAR((3,)),
            dma((4,)),
            dma, dma, dma, dma,
            dma, dma((2,)), dma, dma((2,)),
            dma, dma, dma, dma((4,)),
            dma, dma((4,)), dma, dma,
            dma, dma,
        ]
        return pl.pallas_call(
            functools.partial(kernel, zs, gs),
            out_shape=jax.ShapeDtypeStruct((atoms, F), bf16),
            in_specs=[any_ if i in (3, 4, 10, 11) else vmem for i in range(12)],
            out_specs=pl.BlockSpec(memory_space=pltpu.VMEM),
            scratch_shapes=scratch,
            compiler_params=pltpu.CompilerParams(
                collective_id=0, has_side_effects=True, vmem_limit_bytes=60 * 1024 * 1024
            ),
        )(
            features, positions.T, wave_index.T, wave_filter, mix_pair, msg_weight,
            chan_width.reshape(1, F), pair_dist.T, neighbours.T, norm_gain.reshape(1, F), in_weight, out_weight,
        )

    placed = (
        P(("space", "kgrp"), None), P("space", None), P("kgrp", None), P("kgrp", None), P(), P(), P(),
        P(("space", "kgrp"), None), P(("space", "kgrp"), None), P(), P(), P(),
    )
    return jax.shard_map(
        local, mesh=mesh, in_specs=placed, out_specs=P(("space", "kgrp"), None), check_vma=False
    )
```

```python
import functools
import math

import jax
import jax.numpy as jnp
import numpy as np
from jax import lax
from jax.experimental import pallas as pl
from jax.experimental.pallas import tpu as pltpu
from jax.sharding import PartitionSpec as P

MESH = pl.DeviceIdType.MESH
BOX = 16.0
SLAB_STEP = 0.125
F = 128
WB = 12
TN = (((0,), (0,)), ((), ()))
NN = (((1,), (0,)), ((), ()))

def fit_poly():
    r = 0.5 * np.cos(np.pi * (np.arange(4001) + 0.5) / 4001 / 2)
    t = r * r
    cheb = np.polynomial.chebyshev
    sin_p = cheb.Chebyshev.fit(t, math.sqrt(2) * np.sin(np.pi * r) / r, 4, domain=[0.0, 0.25])
    cos_p = cheb.Chebyshev.fit(t, math.sqrt(2) * np.cos(np.pi * r), 4, domain=[0.0, 0.25])
    to = lambda p: tuple(float(v) for v in p.convert(kind=np.polynomial.Polynomial).coef)
    return to(sin_p), to(cos_p)


SIN_C, COS_C = fit_poly()


def cos_sin_turns(u):
    r = u - jnp.round(u)
    t = r * r
    s = t * SIN_C[-1] + SIN_C[-2]
    for coef in SIN_C[-3::-1]:
        s = s * t + coef
    s = s * r
    c = t * COS_C[-1] + COS_C[-2]
    for coef in COS_C[-3::-1]:
        c = c * t + coef
    return 1.0 - s * s, s * c


def split3(v):
    hi = v.astype(jnp.bfloat16).astype(jnp.float32)
    mid = (v - hi).astype(jnp.bfloat16).astype(jnp.float32)
    return jnp.concatenate([hi, mid, v - hi - mid], axis=0).astype(jnp.bfloat16)


def low_rows(shape):
    return lax.broadcasted_iota(jnp.int32, shape, len(shape) - 2) < 4


def to_blocks(re, im):
    pairs = re.shape[0] // (2 * WB)
    a = re.reshape(pairs, 3, 8, F)
    b = im.reshape(pairs, 3, 8, F)
    a0, a1, a2 = a[:, 0], a[:, 1], a[:, 2]
    b0, b1, b2 = b[:, 0], b[:, 1], b[:, 2]
    low = low_rows(a1.shape)
    x = jnp.where(low, a1, pltpu.roll(b1, 4, 1))
    y = jnp.where(low, pltpu.roll(a1, 4, 1), b1)
    first = jnp.stack([a0, b0, x], axis=1)
    second = jnp.stack([a2, b2, y], axis=1)
    return jnp.stack([first, second], axis=1).reshape(2 * pairs, 3, 8, F)


def from_blocks(v):
    pairs = v.shape[0] // 2
    v = v.reshape(pairs, 2, 3, 8, F)
    x, y = v[:, 0, 2], v[:, 1, 2]
    low = low_rows(x.shape)
    a1 = jnp.where(low, x, pltpu.roll(y, 4, 1))
    b1 = jnp.where(low, pltpu.roll(x, 4, 1), y)
    re = jnp.stack([v[:, 0, 0], a1, v[:, 1, 0]], axis=1).reshape(pairs * 24, F)
    im = jnp.stack([v[:, 0, 1], b1, v[:, 1, 1]], axis=1).reshape(pairs * 24, F)
    return re, im


def far_first(n):
    return sorted(range(1, n), key=lambda o: -min(o, n - o))


def group_order(n):
    nx = min(4, n)
    hops = lambda j: 2 * (j // nx) + min(j % nx, nx - j % nx)
    back = [j // nx * nx + (nx - j % nx) % nx for j in range(n)]
    return nx, sorted(range(1, n), key=lambda j: -hops(j)), back


def slot_of(o, n):
    return 0 if o == 0 else 2 * o - 1 if o <= n // 2 else 2 * (n - o)


def kernel(
    zs, gs, feat, pos, wave, filt, mix, msgw, width, dist, nbr, gain, inw, outw, out,
    fall, halo, ut, pt, pcs, stage, acc, sc_buf, rc_buf, sy_buf, ry_buf, sz_buf, rz_buf,
    ysrc, yall, yv, es, er, msg_t, fil_v, mix_v, inw_v, outw_v,
    know, in_s, ag_s, ag_r, ha_s, ha_r, c_s, c_r, y_s, y_r, z_s, z_r, zb_s, zb_r, yb_s, yb_r, cb_s, cb_r, e_s, e_r,
):
    f32, bf16 = jnp.float32, jnp.bfloat16
    dot = functools.partial(lax.dot_general, preferred_element_type=f32)
    me_s, me_g = lax.axis_index("space"), lax.axis_index("kgrp")
    z, yl, c = me_s // 4, lax.rem(me_s // 2, 2), lax.rem(me_s, 2)
    n_dev = 4 * zs * gs
    flat = me_s * gs + me_g
    up, down = lax.rem(flat + 1, n_dev), lax.rem(flat + n_dev - 1, n_dev)
    up = (up // gs, lax.rem(up, gs))
    down = (down // gs, lax.rem(down, gs))
    nx, group_far, group_back = group_order(gs)
    row, col = me_g // nx, lax.rem(me_g, nx)
    group = [(me_s, lax.rem(row + j // nx, gs // nx) * nx + lax.rem(col + j % nx, nx)) for j in range(gs)]
    core = (z * 4 + yl * 2 + 1 - c, me_g)
    ypeer = (z * 4 + (1 - yl) * 2 + c, me_g)
    ring_z = [lax.rem(z + o, zs) for o in range(zs)]
    ring = [(at * 4 + yl * 2 + c, me_g) for at in ring_z]
    offset_of = sorted(range(zs), key=lambda o: slot_of(o, zs))
    atoms = feat.shape[0]
    kw = wave.shape[1]
    rows = kw // 4

    def remote(src, dst, send, recv, device):
        return pltpu.make_async_remote_copy(
            src_ref=src, dst_ref=dst, send_sem=send, recv_sem=recv, device_id=device, device_id_type=MESH
        )

    def signal(sem, device):
        pl.semaphore_signal(sem, inc=1, device_id=device, device_id_type=MESH)

    barrier = pltpu.get_barrier_semaphore()
    peers = group[1:] + [up, down, core, ypeer, ring[1], ring[zs - 1]]
    for device in peers:
        signal(barrier, device)

    pair = ((c * 2 + yl) * zs + z) // 2
    fetch = [
        pltpu.make_async_copy(src, dst, in_s.at[i])
        for i, (src, dst) in enumerate(
            ((filt.at[pl.ds(pl.multiple_of(pair * 24, 8), 24)], fil_v), (mix, mix_v), (inw, inw_v), (outw, outw_v))
        )
    ]
    for copy in fetch:
        copy.start()

    turned = [pos[:, pl.ds(pl.multiple_of(at * atoms, atoms), atoms)] for _, at in group]
    scales = lax.broadcasted_iota(jnp.int32, pos.shape, 0)
    scales = jnp.where(scales < 2, 1.0 / BOX, 1.0 / (n_dev * atoms * SLAB_STEP)).astype(f32)
    pieces = split3(jnp.concatenate(turned, axis=1) * scales)
    counts = wave[...].astype(f32)
    counts = jnp.concatenate([counts, counts, counts], axis=0).astype(bf16)

    pl.semaphore_wait(barrier, len(peers))

    for j in group_far:
        remote(feat, fall.at[group_back[j]], ag_s, ag_r, group[j]).start()
    edge = atoms // 4
    remote(feat.at[pl.ds(atoms - edge, edge)], halo.at[0], ha_s, ha_r, up).start()
    remote(feat.at[pl.ds(0, edge)], halo.at[1], ha_s, ha_r, down).start()
    fall[0] = feat[...]

    def received(ref, sem):
        remote(ref, ref, ag_s, sem, core).wait_recv()

    def sent(ref, sem):
        remote(ref, ref, sem, ag_r, core).wait_send()

    steps = []
    reach = 1
    while reach < zs // 2:
        steps.append(reach)
        reach *= 2

    def tell(i):
        if i < len(steps):
            signal(know.at[i], ring[steps[i]])
            signal(know.at[i], ring[zs - steps[i]])

    def hear(i):
        if i < len(steps):
            pl.semaphore_wait(know.at[i], 2)

    tell(0)

    chunk = 16 if rows % 16 == 0 else 8
    dom = gs * atoms
    ut[0:kw, 0:dom] = dot(counts, pieces, TN)

    @pl.loop(0, kw // chunk)
    def _(i):
        at = pl.ds(pl.multiple_of(i * chunk, chunk), chunk)
        cos_v, sin_v = cos_sin_turns(ut[at, 0:dom])
        quarter = i // (rows // chunk)
        at = pl.ds(pl.multiple_of(lax.rem(i, rows // chunk) * chunk, chunk), chunk)
        pt[quarter, 0, at, :] = cos_v.astype(bf16)
        pt[quarter, 1, at, :] = sin_v.astype(bf16)

    hear(0)
    tell(1)
    hear(1)
    tell(2)
    if gs > 1:
        received(fall.at[pl.ds(1, gs - 1)], ag_r)

    feats = fall[...].reshape(gs * atoms, F)

    def structure(core_at, y_at):
        sums = dot(pt[core_at * 2 + y_at].reshape(2 * rows, dom), feats, NN)
        stage[...] = to_blocks(sums[:rows], sums[rows:])
        return [stage[pl.ds(ring_z[o], 1)][0] for o in offset_of]

    for i, y_at in enumerate((1 - yl, yl)):
        for s, v in enumerate(structure(1 - c, y_at)):
            sc_buf[i, s] = v.astype(bf16)
        remote(sc_buf.at[i], rc_buf.at[i], c_s, c_r.at[i], core).start()
    cut = zs // 2
    parts = ((cut, zs), (0, cut))
    mine = structure(c, 1 - yl)
    received(rc_buf.at[0], c_r.at[0])
    for i, (lo, hi) in enumerate(parts):
        for s in range(lo, hi):
            sy_buf[s] = (mine[s] + rc_buf[0, s].astype(f32)).astype(bf16)
        part = pl.ds(lo, hi - lo)
        remote(sy_buf.at[part], ry_buf.at[part], y_s, y_r.at[i], ypeer).start()
    mine = structure(c, yl)
    received(rc_buf.at[1], c_r.at[1])
    for s in range(zs):
        acc[s] = mine[s] + rc_buf[1, s].astype(f32)
    hear(2)
    for i, (lo, hi) in enumerate(parts):
        received(ry_buf.at[pl.ds(lo, hi - lo)], y_r.at[i])
        for s in range(hi - 1, lo - 1, -1):
            total = acc[s] + ry_buf[s].astype(f32)
            if s == 0:
                acc[0] = total
                continue
            sz_buf[s] = total.astype(bf16)
            o = offset_of[s]
            remote(sz_buf.at[s], rz_buf.at[slot_of(zs - o, zs)], z_s, z_r, ring[o]).start()

    for copy in fetch:
        copy.wait()
    total = acc[0]
    others = pl.ds(1, zs - 1)
    received(rz_buf.at[others], z_r)
    for s in range(1, zs):
        total = total + rz_buf[s].astype(f32)

    a = (total * (1.0 / math.sqrt(n_dev * atoms))).reshape(24, F).astype(bf16)
    r0 = dot(a, mix_v[0], NN).reshape(3, 8, F)
    r1 = dot(a, mix_v[1], NN).reshape(3, 8, F)
    odd = lax.rem(z, 2) == 1
    fil = fil_v[...].reshape(3, 8, F)
    low = low_rows((8, F))
    swapped = pltpu.roll(fil[1], 4, 0)
    f_main = jnp.where(odd, fil[2], fil[0])
    f_mixed = jnp.where(jnp.logical_xor(low, odd), fil[1], swapped)
    r1_swapped = pltpu.roll(r1[2], 4, 0)
    y_val = jnp.stack(
        [
            f_main * (r0[0] - r1[1]),
            f_main * (r1[0] + r0[1]),
            f_mixed * jnp.where(low, r0[2] - r1_swapped, r0[2] + r1_swapped),
        ],
        axis=0,
    ).astype(bf16)
    ysrc[...] = y_val
    here = c * 2 + yl
    beside = c * 2 + 1 - yl
    cuts = (0, 5, 9, 13, 16) if zs == 16 else (0, zs // 2, zs)
    for o in far_first(zs):
        s = slot_of(zs - o, zs)
        part = sum(s >= hi for hi in cuts[1:])
        remote(ysrc, yall.at[here, s], zb_s, zb_r.at[part], ring[o]).start()
    yall[pl.ds(here, 1), 0] = y_val[None]

    ut[0:dom, 0:kw] = dot(pieces, counts, TN)

    @pl.loop(0, dom // 16)
    def _(i):
        at = pl.ds(pl.multiple_of(i * 16, 16), 16)
        cos_v, sin_v = cos_sin_turns(ut[at, 0:kw])
        pcs[at, 0:kw] = cos_v.astype(bf16)
        pcs[at, kw : 2 * kw] = sin_v.astype(bf16)

    received(halo, ha_r)
    weight = msgw[...]
    ext = jnp.concatenate(
        [
            dot(halo[0], weight, NN),
            dot(feat[...], weight, NN),
            dot(halo[1], weight, NN),
            jnp.zeros((edge * 2, F), f32),
        ],
        axis=0,
    )
    ext_t = ext.T.astype(bf16)
    inv_width = (1.0 / jnp.broadcast_to(width[...], (F, F))).T
    row_ids = lax.broadcasted_iota(jnp.int32, (2 * atoms, atoms), 0)
    message = jnp.zeros((F, atoms), f32)
    for j in range(nbr.shape[0]):
        hot = jnp.where(row_ids == nbr[j : j + 1, :], 1.0, 0.0).astype(bf16)
        near = dot(ext_t, hot, NN)
        message = message + jnp.exp(-(dist[j : j + 1, :] * inv_width)) * near
    msg_t[...] = message.T

    for i in range(len(cuts) - 1):
        lo, hi = cuts[i], cuts[i + 1]
        if hi > max(lo, 1):
            received(yall.at[here, pl.ds(max(lo, 1), hi - max(lo, 1))], zb_r.at[i])
        here_part = yall.at[here, pl.ds(lo, hi - lo)]
        remote(here_part, here_part, yb_s, yb_r.at[i], ypeer).start()
        remote(here_part, here_part, cb_s, cb_r, core).start()
    for i in range(len(cuts) - 1):
        beside_part = yall.at[beside, pl.ds(cuts[i], cuts[i + 1] - cuts[i])]
        received(beside_part, yb_r.at[i])
        remote(beside_part, beside_part, cb_s, cb_r, core).start()
    received(yall.at[pl.ds((1 - c) * 2, 2)], cb_r)

    slots = []
    for t in range(zs):
        o = lax.rem(t - z + zs, zs)
        slots.append(jnp.where(o <= zs // 2, jnp.maximum(2 * o - 1, 0), 2 * (zs - o)))
    for q in range(4):
        blocks = [yall[q, pl.ds(slots[t], 1)] for t in range(zs)]
        re, im = from_blocks(jnp.concatenate(blocks, axis=0).astype(f32))
        yv[q * rows : (q + 1) * rows, :] = re.astype(bf16)
        yv[kw + q * rows : kw + (q + 1) * rows, :] = im.astype(bf16)
    inv_scale = 1.0 / math.sqrt(kw * gs)

    def terms(o):
        return dot(pcs[o * atoms : (o + 1) * atoms, :], yv[...], NN) * inv_scale

    for j in group_far:
        es[j] = terms(j).astype(bf16)
        remote(es.at[j], er.at[group_back[j]], e_s, e_r, group[j]).start()
    ewald = terms(0)

    sent(halo, ha_s)
    sent(sc_buf, c_s)
    sent(sy_buf, y_s)
    sent(sz_buf.at[others], z_s)
    sent(yall.at[here, others], zb_s)
    sent(yall.at[here], yb_s)
    sent(yall.at[pl.ds(c * 2, 2)], cb_s)
    if gs > 1:
        rest = pl.ds(1, gs - 1)
        sent(fall.at[rest], ag_s)
        received(er.at[rest], e_r)
        sent(es.at[rest], e_s)
    for o in range(1, gs):
        ewald = ewald + er[o].astype(f32)

    mixed = feat[...].astype(f32) + msg_t[...] + ewald
    inverse = lax.rsqrt(jnp.mean(mixed * mixed, axis=1, keepdims=True) + 1e-06)
    normed = (mixed * inverse * gain[...]).astype(bf16)
    pre = dot(normed, inw_v[...], NN)
    hidden = (pre * (1.0 / (1.0 + jnp.exp(-pre)))).astype(bf16)
    out[...] = (mixed + dot(hidden, outw_v[...], NN)).astype(bf16)


def solution(mesh):
    zs, gs = mesh.shape["space"] // 4, mesh.shape["kgrp"]

    def local(features, positions, wave_index, wave_filter, mix_pair, msg_weight, chan_width, pair_dist,
              neighbours, norm_gain, in_weight, out_weight):
        atoms = features.shape[0]
        dom = gs * atoms
        kw = wave_index.shape[0]
        f32, bf16 = jnp.float32, jnp.bfloat16
        blk = (3, 8, F)
        big = max(kw, dom)
        vm = pltpu.VMEM
        any_, vmem = pl.BlockSpec(memory_space=pl.ANY), pl.BlockSpec(memory_space=pltpu.VMEM)
        dma = pltpu.SemaphoreType.DMA
        scratch = [
            vm((gs, atoms, F), bf16),
            vm((2, atoms // 4, F), bf16),
            vm((big, big), f32),
            vm((4, 2, kw // 4, dom), bf16),
            vm((dom, 2 * kw), bf16),
            vm((zs, *blk), f32),
            vm((zs, *blk), f32),
            vm((2, zs, *blk), bf16),
            vm((2, zs, *blk), bf16),
            vm((zs, *blk), bf16),
            vm((zs, *blk), bf16),
            vm((zs, *blk), bf16),
            vm((zs, *blk), bf16),
            vm(blk, bf16),
            vm((4, zs, *blk), bf16),
            vm((2 * kw, F), bf16),
            vm((gs, atoms, F), bf16),
            vm((gs, atoms, F), bf16),
            vm((atoms, F), f32),
            vm((2 * WB, F), f32),
            vm(mix_pair.shape, bf16),
            vm(in_weight.shape, bf16),
            vm(out_weight.shape, bf16),
            pltpu.SemaphoreType.REGULAR((3,)),
            dma((4,)),
            dma, dma, dma, dma,
            dma, dma((2,)), dma, dma((2,)),
            dma, dma, dma, dma((4,)),
            dma, dma((4,)), dma, dma,
            dma, dma,
        ]
        return pl.pallas_call(
            functools.partial(kernel, zs, gs),
            out_shape=jax.ShapeDtypeStruct((atoms, F), bf16),
            in_specs=[any_ if i in (3, 4, 10, 11) else vmem for i in range(12)],
            out_specs=pl.BlockSpec(memory_space=pltpu.VMEM),
            scratch_shapes=scratch,
            compiler_params=pltpu.CompilerParams(
                collective_id=0, has_side_effects=True, vmem_limit_bytes=60 * 1024 * 1024
            ),
        )(
            features, positions.T, wave_index.T, wave_filter, mix_pair, msg_weight,
            chan_width.reshape(1, F), pair_dist.T, neighbours.T, norm_gain.reshape(1, F), in_weight, out_weight,
        )

    placed = (
        P(("space", "kgrp"), None), P("space", None), P("kgrp", None), P("kgrp", None), P(), P(), P(),
        P(("space", "kgrp"), None), P(("space", "kgrp"), None), P(), P(), P(),
    )
    return jax.shard_map(
        local, mesh=mesh, in_specs=placed, out_specs=P(("space", "kgrp"), None), check_vma=False
    )
```

```python
import functools
import math

import jax
import jax.numpy as jnp
import numpy as np
from jax import lax
from jax.experimental import pallas as pl
from jax.experimental.pallas import tpu as pltpu
from jax.sharding import PartitionSpec as P

MESH = pl.DeviceIdType.MESH
BOX = 16.0
SLAB_STEP = 0.125
F = 128
WB = 12
TN = (((0,), (0,)), ((), ()))
NN = (((1,), (0,)), ((), ()))

def fit_poly():
    r = 0.5 * np.cos(np.pi * (np.arange(4001) + 0.5) / 4001 / 2)
    t = r * r
    cheb = np.polynomial.chebyshev
    sin_p = cheb.Chebyshev.fit(t, math.sqrt(2) * np.sin(np.pi * r) / r, 4, domain=[0.0, 0.25])
    cos_p = cheb.Chebyshev.fit(t, math.sqrt(2) * np.cos(np.pi * r), 4, domain=[0.0, 0.25])
    to = lambda p: tuple(float(v) for v in p.convert(kind=np.polynomial.Polynomial).coef)
    return to(sin_p), to(cos_p)


SIN_C, COS_C = fit_poly()


def cos_sin_turns(u):
    r = u - jnp.round(u)
    t = r * r
    s = t * SIN_C[-1] + SIN_C[-2]
    for coef in SIN_C[-3::-1]:
        s = s * t + coef
    s = s * r
    c = t * COS_C[-1] + COS_C[-2]
    for coef in COS_C[-3::-1]:
        c = c * t + coef
    return 1.0 - s * s, s * c


def split3(v):
    hi = v.astype(jnp.bfloat16).astype(jnp.float32)
    mid = (v - hi).astype(jnp.bfloat16).astype(jnp.float32)
    return jnp.concatenate([hi, mid, v - hi - mid], axis=0).astype(jnp.bfloat16)


def low_rows(shape):
    return lax.broadcasted_iota(jnp.int32, shape, len(shape) - 2) < 4


def to_blocks(re, im):
    pairs = re.shape[0] // (2 * WB)
    a = re.reshape(pairs, 3, 8, F)
    b = im.reshape(pairs, 3, 8, F)
    a0, a1, a2 = a[:, 0], a[:, 1], a[:, 2]
    b0, b1, b2 = b[:, 0], b[:, 1], b[:, 2]
    low = low_rows(a1.shape)
    x = jnp.where(low, a1, pltpu.roll(b1, 4, 1))
    y = jnp.where(low, pltpu.roll(a1, 4, 1), b1)
    first = jnp.stack([a0, b0, x], axis=1)
    second = jnp.stack([a2, b2, y], axis=1)
    return jnp.stack([first, second], axis=1).reshape(2 * pairs, 3, 8, F)


def from_blocks(v):
    pairs = v.shape[0] // 2
    v = v.reshape(pairs, 2, 3, 8, F)
    x, y = v[:, 0, 2], v[:, 1, 2]
    low = low_rows(x.shape)
    a1 = jnp.where(low, x, pltpu.roll(y, 4, 1))
    b1 = jnp.where(low, pltpu.roll(x, 4, 1), y)
    re = jnp.stack([v[:, 0, 0], a1, v[:, 1, 0]], axis=1).reshape(pairs * 24, F)
    im = jnp.stack([v[:, 0, 1], b1, v[:, 1, 1]], axis=1).reshape(pairs * 24, F)
    return re, im


def far_first(n):
    return sorted(range(1, n), key=lambda o: -min(o, n - o))


def group_order(n):
    nx = min(4, n)
    hops = lambda j: 2 * (j // nx) + min(j % nx, nx - j % nx)
    back = [j // nx * nx + (nx - j % nx) % nx for j in range(n)]
    return nx, sorted(range(1, n), key=lambda j: -hops(j)), back


def slot_of(o, n):
    return 0 if o == 0 else 2 * o - 1 if o <= n // 2 else 2 * (n - o)


def kernel(
    zs, gs, feat_h, pos_h, wave_h, filt_h, mix_h, msgw_h, width_h, dist_h, nbr_h, gain_h, inw_h, outw_h, out,
    fall, halo, ut, pt, pcs, stage, acc, sc_buf, rc_buf, sy_buf, ry_buf, sz_buf, rz_buf,
    ysrc, yall, yv, es, er, msg_t, feat, pos, wave, filt, mix, msgw, width, dist, nbr, gain, inw, outw,
    know, in_s, ag_s, ag_r, ha_s, ha_r, c_s, c_r, y_s, y_r, z_s, z_r, zb_s, zb_r, yb_s, yb_r, e_s, e_r,
):
    f32, bf16 = jnp.float32, jnp.bfloat16
    dot = functools.partial(lax.dot_general, preferred_element_type=f32)
    me_s, me_g = lax.axis_index("space"), lax.axis_index("kgrp")
    z, yl, c = me_s // 4, lax.rem(me_s // 2, 2), lax.rem(me_s, 2)
    n_dev = 4 * zs * gs
    flat = me_s * gs + me_g
    up, down = lax.rem(flat + 1, n_dev), lax.rem(flat + n_dev - 1, n_dev)
    up = (up // gs, lax.rem(up, gs))
    down = (down // gs, lax.rem(down, gs))
    nx, group_far, group_back = group_order(gs)
    row, col = me_g // nx, lax.rem(me_g, nx)
    group = [(me_s, lax.rem(row + j // nx, gs // nx) * nx + lax.rem(col + j % nx, nx)) for j in range(gs)]
    core = (z * 4 + yl * 2 + 1 - c, me_g)
    ypeer = (z * 4 + (1 - yl) * 2 + c, me_g)
    diagonal = (z * 4 + (1 - yl) * 2 + 1 - c, me_g)
    ring_z = [lax.rem(z + o, zs) for o in range(zs)]
    ring = [(at * 4 + yl * 2 + c, me_g) for at in ring_z]
    offset_of = sorted(range(zs), key=lambda o: slot_of(o, zs))
    atoms = feat.shape[0]
    kw = wave.shape[1]
    rows = kw // 4

    def remote(src, dst, send, recv, device):
        return pltpu.make_async_remote_copy(
            src_ref=src, dst_ref=dst, send_sem=send, recv_sem=recv, device_id=device, device_id_type=MESH
        )

    def signal(sem, device):
        pl.semaphore_signal(sem, inc=1, device_id=device, device_id_type=MESH)

    barrier = pltpu.get_barrier_semaphore()
    peers = group[1:] + [up, down, core, ypeer, diagonal, ring[1], ring[zs - 1]]
    for device in peers:
        signal(barrier, device)

    pair = ((c * 2 + yl) * zs + z) // 2
    filt_part = filt_h.at[pl.ds(pl.multiple_of(pair * 24, 8), 24)]
    fetch = [
        pltpu.make_async_copy(src, dst, in_s.at[i])
        for i, (src, dst) in enumerate(
            (
                (pos_h, pos), (wave_h, wave), (feat_h, feat), (filt_part, filt), (mix_h, mix), (msgw_h, msgw),
                (width_h, width), (dist_h, dist), (nbr_h, nbr), (gain_h, gain), (inw_h, inw), (outw_h, outw),
            )
        )
    ]
    for copy in fetch:
        copy.start()
    fetch[0].wait()
    fetch[1].wait()

    turned = [pos[:, pl.ds(pl.multiple_of(at * atoms, atoms), atoms)] for _, at in group]
    scales = lax.broadcasted_iota(jnp.int32, pos.shape, 0)
    scales = jnp.where(scales < 2, 1.0 / BOX, 1.0 / (n_dev * atoms * SLAB_STEP)).astype(f32)
    pieces = split3(jnp.concatenate(turned, axis=1) * scales)
    counts = wave[...].astype(f32)
    counts = jnp.concatenate([counts, counts, counts], axis=0).astype(bf16)

    fetch[2].wait()
    pl.semaphore_wait(barrier, len(peers))

    for j in group_far:
        remote(feat, fall.at[group_back[j]], ag_s, ag_r, group[j]).start()
    edge = atoms // 4
    remote(feat.at[pl.ds(atoms - edge, edge)], halo.at[0], ha_s, ha_r, up).start()
    remote(feat.at[pl.ds(0, edge)], halo.at[1], ha_s, ha_r, down).start()
    fall[0] = feat[...]

    def received(ref, sem):
        remote(ref, ref, ag_s, sem, core).wait_recv()

    def sent(ref, sem):
        remote(ref, ref, sem, ag_r, core).wait_send()

    steps = []
    reach = 1
    while reach < zs // 2:
        steps.append(reach)
        reach *= 2

    def tell(i):
        if i < len(steps):
            signal(know.at[i], ring[steps[i]])
            signal(know.at[i], ring[zs - steps[i]])

    def hear(i):
        if i < len(steps):
            pl.semaphore_wait(know.at[i], 2)

    tell(0)

    chunk = 16 if rows % 16 == 0 else 8
    dom = gs * atoms
    ut[0:kw, 0:dom] = dot(counts, pieces, TN)

    @pl.loop(0, kw // chunk)
    def _(i):
        at = pl.ds(pl.multiple_of(i * chunk, chunk), chunk)
        cos_v, sin_v = cos_sin_turns(ut[at, 0:dom])
        quarter = i // (rows // chunk)
        at = pl.ds(pl.multiple_of(lax.rem(i, rows // chunk) * chunk, chunk), chunk)
        pt[quarter, 0, at, :] = cos_v.astype(bf16)
        pt[quarter, 1, at, :] = sin_v.astype(bf16)

    hear(0)
    tell(1)
    hear(1)
    tell(2)
    if gs > 1:
        received(fall.at[pl.ds(1, gs - 1)], ag_r)

    feats = fall[...].reshape(gs * atoms, F)

    def structure(core_at, y_at):
        sums = dot(pt[core_at * 2 + y_at].reshape(2 * rows, dom), feats, NN)
        stage[...] = to_blocks(sums[:rows], sums[rows:])
        return [stage[pl.ds(ring_z[o], 1)][0] for o in offset_of]

    for i, y_at in enumerate((1 - yl, yl)):
        for s, v in enumerate(structure(1 - c, y_at)):
            sc_buf[i, s] = v.astype(bf16)
        remote(sc_buf.at[i], rc_buf.at[i], c_s, c_r.at[i], core).start()
    cut = zs // 2
    parts = ((cut, zs), (0, cut))
    mine = structure(c, 1 - yl)
    received(rc_buf.at[0], c_r.at[0])
    for i, (lo, hi) in enumerate(parts):
        for s in range(lo, hi):
            sy_buf[s] = (mine[s] + rc_buf[0, s].astype(f32)).astype(bf16)
        part = pl.ds(lo, hi - lo)
        remote(sy_buf.at[part], ry_buf.at[part], y_s, y_r.at[i], ypeer).start()
    mine = structure(c, yl)
    received(rc_buf.at[1], c_r.at[1])
    for s in range(zs):
        acc[s] = mine[s] + rc_buf[1, s].astype(f32)
    hear(2)
    for i, (lo, hi) in enumerate(parts):
        received(ry_buf.at[pl.ds(lo, hi - lo)], y_r.at[i])
        for s in range(hi - 1, lo - 1, -1):
            total = acc[s] + ry_buf[s].astype(f32)
            if s == 0:
                acc[0] = total
                continue
            sz_buf[s] = total.astype(bf16)
            o = offset_of[s]
            remote(sz_buf.at[s], rz_buf.at[slot_of(zs - o, zs)], z_s, z_r, ring[o]).start()

    for copy in fetch[3:]:
        copy.wait()
    total = acc[0]
    others = pl.ds(1, zs - 1)
    received(rz_buf.at[others], z_r)
    for s in range(1, zs):
        total = total + rz_buf[s].astype(f32)

    a = (total * (1.0 / math.sqrt(n_dev * atoms))).reshape(24, F).astype(bf16)
    r0 = dot(a, mix[0], NN).reshape(3, 8, F)
    r1 = dot(a, mix[1], NN).reshape(3, 8, F)
    odd = lax.rem(z, 2) == 1
    fil = filt[...].reshape(3, 8, F)
    low = low_rows((8, F))
    swapped = pltpu.roll(fil[1], 4, 0)
    f_main = jnp.where(odd, fil[2], fil[0])
    f_mixed = jnp.where(jnp.logical_xor(low, odd), fil[1], swapped)
    r1_swapped = pltpu.roll(r1[2], 4, 0)
    y_val = jnp.stack(
        [
            f_main * (r0[0] - r1[1]),
            f_main * (r1[0] + r0[1]),
            f_mixed * jnp.where(low, r0[2] - r1_swapped, r0[2] + r1_swapped),
        ],
        axis=0,
    ).astype(bf16)
    ysrc[...] = y_val
    here = c * 2 + yl
    cuts = (0, 5, 9, 13, 16) if zs == 16 else (0, zs // 2, zs)
    for o in far_first(zs):
        s = slot_of(zs - o, zs)
        part = sum(s >= hi for hi in cuts[1:])
        remote(ysrc, yall.at[here, s], zb_s, zb_r.at[part], ring[o]).start()
    yall[pl.ds(here, 1), 0] = y_val[None]

    ut[0:dom, 0:kw] = dot(pieces, counts, TN)

    @pl.loop(0, dom // 16)
    def _(i):
        at = pl.ds(pl.multiple_of(i * 16, 16), 16)
        cos_v, sin_v = cos_sin_turns(ut[at, 0:kw])
        pcs[at, 0:kw] = cos_v.astype(bf16)
        pcs[at, kw : 2 * kw] = sin_v.astype(bf16)

    received(halo, ha_r)
    weight = msgw[...]
    ext = jnp.concatenate(
        [
            dot(halo[0], weight, NN),
            dot(feat[...], weight, NN),
            dot(halo[1], weight, NN),
            jnp.zeros((edge * 2, F), f32),
        ],
        axis=0,
    )
    ext_t = ext.T.astype(bf16)
    inv_width = (1.0 / jnp.broadcast_to(width[...], (F, F))).T
    row_ids = lax.broadcasted_iota(jnp.int32, (2 * atoms, atoms), 0)
    message = jnp.zeros((F, atoms), f32)
    for j in range(nbr.shape[0]):
        hot = jnp.where(row_ids == nbr[j : j + 1, :], 1.0, 0.0).astype(bf16)
        near = dot(ext_t, hot, NN)
        message = message + jnp.exp(-(dist[j : j + 1, :] * inv_width)) * near
    msg_t[...] = message.T

    for i in range(len(cuts) - 1):
        lo, hi = cuts[i], cuts[i + 1]
        if hi > max(lo, 1):
            received(yall.at[here, pl.ds(max(lo, 1), hi - max(lo, 1))], zb_r.at[i])
        here_part = yall.at[here, pl.ds(lo, hi - lo)]
        for device in (diagonal, ypeer, core):
            remote(here_part, here_part, yb_s, yb_r, device).start()
    received(yall.at[pl.ds(1, 3)], yb_r)

    slots = []
    for t in range(zs):
        o = lax.rem(t - z + zs, zs)
        slots.append(jnp.where(o <= zs // 2, jnp.maximum(2 * o - 1, 0), 2 * (zs - o)))
    for q in range(4):
        blocks = [yall[q, pl.ds(slots[t], 1)] for t in range(zs)]
        re, im = from_blocks(jnp.concatenate(blocks, axis=0).astype(f32))
        yv[q * rows : (q + 1) * rows, :] = re.astype(bf16)
        yv[kw + q * rows : kw + (q + 1) * rows, :] = im.astype(bf16)
    inv_scale = 1.0 / math.sqrt(kw * gs)

    def terms(o):
        return dot(pcs[o * atoms : (o + 1) * atoms, :], yv[...], NN) * inv_scale

    for j in group_far:
        es[j] = terms(j).astype(bf16)
        remote(es.at[j], er.at[group_back[j]], e_s, e_r, group[j]).start()
    ewald = terms(0)

    sent(halo, ha_s)
    sent(sc_buf, c_s)
    sent(sy_buf, y_s)
    sent(sz_buf.at[others], z_s)
    sent(yall.at[here, others], zb_s)
    sent(yall.at[pl.ds(1, 3)], yb_s)
    if gs > 1:
        rest = pl.ds(1, gs - 1)
        sent(fall.at[rest], ag_s)
        received(er.at[rest], e_r)
        sent(es.at[rest], e_s)
    for o in range(1, gs):
        ewald = ewald + er[o].astype(f32)

    mixed = feat[...].astype(f32) + msg_t[...] + ewald
    inverse = lax.rsqrt(jnp.mean(mixed * mixed, axis=1, keepdims=True) + 1e-06)
    normed = (mixed * inverse * gain[...]).astype(bf16)
    pre = dot(normed, inw[...], NN)
    hidden = (pre * (1.0 / (1.0 + jnp.exp(-pre)))).astype(bf16)
    out[...] = (mixed + dot(hidden, outw[...], NN)).astype(bf16)


def solution(mesh):
    zs, gs = mesh.shape["space"] // 4, mesh.shape["kgrp"]

    def local(features, positions, wave_index, wave_filter, mix_pair, msg_weight, chan_width, pair_dist,
              neighbours, norm_gain, in_weight, out_weight):
        atoms = features.shape[0]
        dom = gs * atoms
        kw = wave_index.shape[0]
        f32, bf16 = jnp.float32, jnp.bfloat16
        blk = (3, 8, F)
        big = max(kw, dom)
        vm = pltpu.VMEM
        dma = pltpu.SemaphoreType.DMA
        scratch = [
            vm((gs, atoms, F), bf16),
            vm((2, atoms // 4, F), bf16),
            vm((big, big), f32),
            vm((4, 2, kw // 4, dom), bf16),
            vm((dom, 2 * kw), bf16),
            vm((zs, *blk), f32),
            vm((zs, *blk), f32),
            vm((2, zs, *blk), bf16),
            vm((2, zs, *blk), bf16),
            vm((zs, *blk), bf16),
            vm((zs, *blk), bf16),
            vm((zs, *blk), bf16),
            vm((zs, *blk), bf16),
            vm(blk, bf16),
            vm((4, zs, *blk), bf16),
            vm((2 * kw, F), bf16),
            vm((gs, atoms, F), bf16),
            vm((gs, atoms, F), bf16),
            vm((atoms, F), f32),
            vm((atoms, F), bf16),
            vm((3, dom), f32),
            vm((3, kw), jnp.int32),
            vm((2 * WB, F), f32),
            vm(mix_pair.shape, bf16),
            vm(msg_weight.shape, bf16),
            vm((1, F), f32),
            vm(pair_dist.shape[::-1], f32),
            vm(neighbours.shape[::-1], jnp.int32),
            vm((1, F), f32),
            vm(in_weight.shape, bf16),
            vm(out_weight.shape, bf16),
            pltpu.SemaphoreType.REGULAR((3,)),
            dma((12,)),
            dma, dma, dma, dma,
            dma, dma((2,)), dma, dma((2,)),
            dma, dma, dma, dma((4,)),
            dma, dma, dma, dma,
        ]
        return pl.pallas_call(
            functools.partial(kernel, zs, gs),
            out_shape=jax.ShapeDtypeStruct((atoms, F), bf16),
            in_specs=[pl.BlockSpec(memory_space=pl.ANY)] * 12,
            out_specs=pl.BlockSpec(memory_space=pltpu.VMEM),
            scratch_shapes=scratch,
            compiler_params=pltpu.CompilerParams(
                collective_id=0, has_side_effects=True, vmem_limit_bytes=60 * 1024 * 1024
            ),
        )(
            features, positions.T, wave_index.T, wave_filter, mix_pair, msg_weight,
            chan_width.reshape(1, F), pair_dist.T, neighbours.T, norm_gain.reshape(1, F), in_weight, out_weight,
        )

    placed = (
        P(("space", "kgrp"), None), P("space", None), P("kgrp", None), P("kgrp", None), P(), P(), P(),
        P(("space", "kgrp"), None), P(("space", "kgrp"), None), P(), P(), P(),
    )
    return jax.shard_map(
        local, mesh=mesh, in_specs=placed, out_specs=P(("space", "kgrp"), None), check_vma=False
    )
```

```python
import functools
import math

import jax
import jax.numpy as jnp
import numpy as np
from jax import lax
from jax.experimental import pallas as pl
from jax.experimental.pallas import tpu as pltpu
from jax.sharding import PartitionSpec as P

MESH = pl.DeviceIdType.MESH
BOX = 16.0
SLAB_STEP = 0.125
F = 128
WB = 12
TN = (((0,), (0,)), ((), ()))
NN = (((1,), (0,)), ((), ()))

def fit_poly():
    r = 0.5 * np.cos(np.pi * (np.arange(4001) + 0.5) / 4001 / 2)
    t = r * r
    cheb = np.polynomial.chebyshev
    sin_p = cheb.Chebyshev.fit(t, math.sqrt(2) * np.sin(np.pi * r) / r, 4, domain=[0.0, 0.25])
    cos_p = cheb.Chebyshev.fit(t, math.sqrt(2) * np.cos(np.pi * r), 4, domain=[0.0, 0.25])
    to = lambda p: tuple(float(v) for v in p.convert(kind=np.polynomial.Polynomial).coef)
    return to(sin_p), to(cos_p)


SIN_C, COS_C = fit_poly()


def cos_sin_turns(u):
    r = u - jnp.round(u)
    t = r * r
    s = t * SIN_C[-1] + SIN_C[-2]
    for coef in SIN_C[-3::-1]:
        s = s * t + coef
    s = s * r
    c = t * COS_C[-1] + COS_C[-2]
    for coef in COS_C[-3::-1]:
        c = c * t + coef
    return 1.0 - s * s, s * c


def split3(v):
    hi = v.astype(jnp.bfloat16).astype(jnp.float32)
    mid = (v - hi).astype(jnp.bfloat16).astype(jnp.float32)
    return jnp.concatenate([hi, mid, v - hi - mid], axis=0).astype(jnp.bfloat16)


def low_rows(shape):
    return lax.broadcasted_iota(jnp.int32, shape, len(shape) - 2) < 4


def to_blocks(re, im):
    pairs = re.shape[0] // (2 * WB)
    a = re.reshape(pairs, 3, 8, F)
    b = im.reshape(pairs, 3, 8, F)
    a0, a1, a2 = a[:, 0], a[:, 1], a[:, 2]
    b0, b1, b2 = b[:, 0], b[:, 1], b[:, 2]
    low = low_rows(a1.shape)
    x = jnp.where(low, a1, pltpu.roll(b1, 4, 1))
    y = jnp.where(low, pltpu.roll(a1, 4, 1), b1)
    first = jnp.stack([a0, b0, x], axis=1)
    second = jnp.stack([a2, b2, y], axis=1)
    return jnp.stack([first, second], axis=1).reshape(2 * pairs, 3, 8, F)


def from_blocks(v):
    pairs = v.shape[0] // 2
    v = v.reshape(pairs, 2, 3, 8, F)
    x, y = v[:, 0, 2], v[:, 1, 2]
    low = low_rows(x.shape)
    a1 = jnp.where(low, x, pltpu.roll(y, 4, 1))
    b1 = jnp.where(low, pltpu.roll(x, 4, 1), y)
    re = jnp.stack([v[:, 0, 0], a1, v[:, 1, 0]], axis=1).reshape(pairs * 24, F)
    im = jnp.stack([v[:, 0, 1], b1, v[:, 1, 1]], axis=1).reshape(pairs * 24, F)
    return re, im


def far_first(n):
    return sorted(range(1, n), key=lambda o: -min(o, n - o))


def group_order(n):
    nx = min(4, n)
    hops = lambda j: 2 * (j // nx) + min(j % nx, nx - j % nx)
    back = [j // nx * nx + (nx - j % nx) % nx for j in range(n)]
    return nx, sorted(range(1, n), key=lambda j: -hops(j)), back


def slot_of(o, n):
    return 0 if o == 0 else 2 * o - 1 if o <= n // 2 else 2 * (n - o)


def kernel(
    zs, gs, feat_h, pos_h, wave_h, filt_h, mix_h, msgw_h, width_h, dist_h, nbr_h, gain_h, inw_h, outw_h, out,
    fall, halo, ut, pt, pcs, stage, acc, sc_buf, rc_buf, sz_buf, rz_buf,
    ysrc, yall, yv, es, er, msg_t, feat, pos, wave, filt, mix, msgw, width, dist, nbr, gain, inw, outw,
    know, in_s, ag_s, ag_r, ha_s, ha_r, c_s, c_r, z_s, z_r, zb_s, zb_r, yb_s, yb_r, e_s, e_r,
):
    f32, bf16 = jnp.float32, jnp.bfloat16
    dot = functools.partial(lax.dot_general, preferred_element_type=f32)
    me_s, me_g = lax.axis_index("space"), lax.axis_index("kgrp")
    z, yl, c = me_s // 4, lax.rem(me_s // 2, 2), lax.rem(me_s, 2)
    n_dev = 4 * zs * gs
    flat = me_s * gs + me_g
    up, down = lax.rem(flat + 1, n_dev), lax.rem(flat + n_dev - 1, n_dev)
    up = (up // gs, lax.rem(up, gs))
    down = (down // gs, lax.rem(down, gs))
    nx, group_far, group_back = group_order(gs)
    row, col = me_g // nx, lax.rem(me_g, nx)
    group = [(me_s, lax.rem(row + j // nx, gs // nx) * nx + lax.rem(col + j % nx, nx)) for j in range(gs)]
    core = (z * 4 + yl * 2 + 1 - c, me_g)
    ypeer = (z * 4 + (1 - yl) * 2 + c, me_g)
    diagonal = (z * 4 + (1 - yl) * 2 + 1 - c, me_g)
    ring_z = [lax.rem(z + o, zs) for o in range(zs)]
    ring = [(at * 4 + yl * 2 + c, me_g) for at in ring_z]
    offset_of = sorted(range(zs), key=lambda o: slot_of(o, zs))
    atoms = feat.shape[0]
    kw = wave.shape[1]
    rows = kw // 4

    def remote(src, dst, send, recv, device):
        return pltpu.make_async_remote_copy(
            src_ref=src, dst_ref=dst, send_sem=send, recv_sem=recv, device_id=device, device_id_type=MESH
        )

    def signal(sem, device):
        pl.semaphore_signal(sem, inc=1, device_id=device, device_id_type=MESH)

    barrier = pltpu.get_barrier_semaphore()
    peers = group[1:] + [up, down, core, ypeer, diagonal, ring[1], ring[zs - 1]]
    for device in peers:
        signal(barrier, device)

    pair = ((c * 2 + yl) * zs + z) // 2
    filt_part = filt_h.at[pl.ds(pl.multiple_of(pair * 24, 8), 24)]
    fetch = [
        pltpu.make_async_copy(src, dst, in_s.at[i])
        for i, (src, dst) in enumerate(
            (
                (pos_h, pos), (wave_h, wave), (feat_h, feat), (filt_part, filt), (mix_h, mix), (msgw_h, msgw),
                (width_h, width), (dist_h, dist), (nbr_h, nbr), (gain_h, gain), (inw_h, inw), (outw_h, outw),
            )
        )
    ]
    for copy in fetch:
        copy.start()
    fetch[0].wait()
    fetch[1].wait()

    turned = [pos[:, pl.ds(pl.multiple_of(at * atoms, atoms), atoms)] for _, at in group]
    scales = lax.broadcasted_iota(jnp.int32, pos.shape, 0)
    scales = jnp.where(scales < 2, 1.0 / BOX, 1.0 / (n_dev * atoms * SLAB_STEP)).astype(f32)
    pieces = split3(jnp.concatenate(turned, axis=1) * scales)
    counts = wave[...].astype(f32)
    counts = jnp.concatenate([counts, counts, counts], axis=0).astype(bf16)

    fetch[2].wait()
    pl.semaphore_wait(barrier, len(peers))

    for j in group_far:
        remote(feat, fall.at[group_back[j]], ag_s, ag_r, group[j]).start()
    edge = atoms // 4
    remote(feat.at[pl.ds(atoms - edge, edge)], halo.at[0], ha_s, ha_r, up).start()
    remote(feat.at[pl.ds(0, edge)], halo.at[1], ha_s, ha_r, down).start()
    fall[0] = feat[...]

    def received(ref, sem):
        remote(ref, ref, ag_s, sem, core).wait_recv()

    def sent(ref, sem):
        remote(ref, ref, sem, ag_r, core).wait_send()

    steps = []
    reach = 1
    while reach < zs // 2:
        steps.append(reach)
        reach *= 2

    def tell(i):
        if i < len(steps):
            signal(know.at[i], ring[steps[i]])
            signal(know.at[i], ring[zs - steps[i]])

    def hear(i):
        if i < len(steps):
            pl.semaphore_wait(know.at[i], 2)

    tell(0)

    chunk = 16 if rows % 16 == 0 else 8
    dom = gs * atoms
    ut[0:kw, 0:dom] = dot(counts, pieces, TN)

    @pl.loop(0, kw // chunk)
    def _(i):
        at = pl.ds(pl.multiple_of(i * chunk, chunk), chunk)
        cos_v, sin_v = cos_sin_turns(ut[at, 0:dom])
        quarter = i // (rows // chunk)
        at = pl.ds(pl.multiple_of(lax.rem(i, rows // chunk) * chunk, chunk), chunk)
        pt[quarter, 0, at, :] = cos_v.astype(bf16)
        pt[quarter, 1, at, :] = sin_v.astype(bf16)

    hear(0)
    tell(1)
    hear(1)
    tell(2)
    if gs > 1:
        received(fall.at[pl.ds(1, gs - 1)], ag_r)

    feats = fall[...].reshape(gs * atoms, F)

    def structure(core_at, y_at):
        sums = dot(pt[core_at * 2 + y_at].reshape(2 * rows, dom), feats, NN)
        stage[...] = to_blocks(sums[:rows], sums[rows:])
        return [stage[pl.ds(ring_z[o], 1)][0] for o in offset_of]

    cut = zs // 2
    parts = ((cut, zs), (0, cut))
    quad = (diagonal, ypeer, core)

    def swap(k, i):
        part = pl.ds(parts[i][0], parts[i][1] - parts[i][0])
        remote(sc_buf.at[k, part], rc_buf.at[k, part], c_s, c_r.at[i], quad[k]).start()

    for k, (core_at, y_at) in enumerate(((1 - c, 1 - yl), (c, 1 - yl), (1 - c, yl))):
        for s, v in enumerate(structure(core_at, y_at)):
            sc_buf[k, s] = v.astype(bf16)
        swap(k, 0)
        if k:
            swap(k, 1)
        if k == 1:
            swap(0, 1)
    mine = structure(c, yl)
    hear(2)
    for i, (lo, hi) in enumerate(parts):
        received(rc_buf.at[:, pl.ds(lo, hi - lo)], c_r.at[i])
        for s in range(hi - 1, lo - 1, -1):
            total = mine[s]
            for k in range(3):
                total = total + rc_buf[k, s].astype(f32)
            if s == 0:
                acc[...] = total
                continue
            sz_buf[s] = total.astype(bf16)
            o = offset_of[s]
            remote(sz_buf.at[s], rz_buf.at[slot_of(zs - o, zs)], z_s, z_r, ring[o]).start()

    for copy in fetch[3:]:
        copy.wait()
    total = acc[...]
    others = pl.ds(1, zs - 1)
    received(rz_buf.at[others], z_r)
    for s in range(1, zs):
        total = total + rz_buf[s].astype(f32)

    a = (total * (1.0 / math.sqrt(n_dev * atoms))).reshape(24, F).astype(bf16)
    r0 = dot(a, mix[0], NN).reshape(3, 8, F)
    r1 = dot(a, mix[1], NN).reshape(3, 8, F)
    odd = lax.rem(z, 2) == 1
    fil = filt[...].reshape(3, 8, F)
    low = low_rows((8, F))
    swapped = pltpu.roll(fil[1], 4, 0)
    f_main = jnp.where(odd, fil[2], fil[0])
    f_mixed = jnp.where(jnp.logical_xor(low, odd), fil[1], swapped)
    r1_swapped = pltpu.roll(r1[2], 4, 0)
    y_val = jnp.stack(
        [
            f_main * (r0[0] - r1[1]),
            f_main * (r1[0] + r0[1]),
            f_mixed * jnp.where(low, r0[2] - r1_swapped, r0[2] + r1_swapped),
        ],
        axis=0,
    ).astype(bf16)
    ysrc[...] = y_val
    here = c * 2 + yl
    cuts = (0, 5, 9, 13, 16) if zs == 16 else (0, zs // 2, zs)
    for o in far_first(zs):
        s = slot_of(zs - o, zs)
        part = sum(s >= hi for hi in cuts[1:])
        remote(ysrc, yall.at[here, s], zb_s, zb_r.at[part], ring[o]).start()
    yall[pl.ds(here, 1), 0] = y_val[None]

    send_order = group_far + [0]
    lanes = [pieces[:, j * atoms : (j + 1) * atoms] for j in send_order]
    ut[0:dom, 0:kw] = dot(jnp.concatenate(lanes, axis=1), counts, TN)

    @pl.loop(0, dom // 16)
    def _(i):
        at = pl.ds(pl.multiple_of(i * 16, 16), 16)
        cos_v, sin_v = cos_sin_turns(ut[at, 0:kw])
        pcs[at, 0:kw] = cos_v.astype(bf16)
        pcs[at, kw : 2 * kw] = sin_v.astype(bf16)

    received(halo, ha_r)
    weight = msgw[...]
    ext = jnp.concatenate(
        [
            dot(halo[0], weight, NN),
            dot(feat[...], weight, NN),
            dot(halo[1], weight, NN),
            jnp.zeros((edge * 2, F), f32),
        ],
        axis=0,
    )
    ext_t = ext.T.astype(bf16)
    inv_width = (1.0 / jnp.broadcast_to(width[...], (F, F))).T
    row_ids = lax.broadcasted_iota(jnp.int32, (2 * atoms, atoms), 0)
    message = jnp.zeros((F, atoms), f32)
    for j in range(nbr.shape[0]):
        hot = jnp.where(row_ids == nbr[j : j + 1, :], 1.0, 0.0).astype(bf16)
        near = dot(ext_t, hot, NN)
        message = message + jnp.exp(-(dist[j : j + 1, :] * inv_width)) * near
    msg_t[...] = message.T

    for i in range(len(cuts) - 1):
        lo, hi = cuts[i], cuts[i + 1]
        if hi > max(lo, 1):
            received(yall.at[here, pl.ds(max(lo, 1), hi - max(lo, 1))], zb_r.at[i])
        here_part = yall.at[here, pl.ds(lo, hi - lo)]
        for device in (diagonal, ypeer, core):
            remote(here_part, here_part, yb_s, yb_r, device).start()
    received(yall.at[pl.ds(1, 3)], yb_r)

    slots = []
    for t in range(zs):
        o = lax.rem(t - z + zs, zs)
        slots.append(jnp.where(o <= zs // 2, jnp.maximum(2 * o - 1, 0), 2 * (zs - o)))
    for q in range(4):
        blocks = [yall[q, pl.ds(slots[t], 1)] for t in range(zs)]
        re, im = from_blocks(jnp.concatenate(blocks, axis=0).astype(f32))
        yv[q * rows : (q + 1) * rows, :] = re.astype(bf16)
        yv[kw + q * rows : kw + (q + 1) * rows, :] = im.astype(bf16)
    inv_scale = 1.0 / math.sqrt(kw * gs)

    bounds = (0, 1, 4, 8) if gs == 8 else (0, gs)
    for lo, hi in zip(bounds[:-1], bounds[1:]):
        terms = dot(pcs[lo * atoms : hi * atoms, :], yv[...], NN) * inv_scale
        for i in range(lo, hi):
            j = send_order[i]
            term = terms[(i - lo) * atoms : (i - lo + 1) * atoms]
            if j == 0:
                ewald = term
                continue
            es[j] = term.astype(bf16)
            remote(es.at[j], er.at[group_back[j]], e_s, e_r, group[j]).start()

    sent(halo, ha_s)
    sent(sc_buf, c_s)
    sent(sz_buf.at[others], z_s)
    sent(yall.at[here, others], zb_s)
    sent(yall.at[pl.ds(1, 3)], yb_s)
    if gs > 1:
        rest = pl.ds(1, gs - 1)
        sent(fall.at[rest], ag_s)
        received(er.at[rest], e_r)
        sent(es.at[rest], e_s)
    for o in range(1, gs):
        ewald = ewald + er[o].astype(f32)

    mixed = feat[...].astype(f32) + msg_t[...] + ewald
    inverse = lax.rsqrt(jnp.mean(mixed * mixed, axis=1, keepdims=True) + 1e-06)
    normed = (mixed * inverse * gain[...]).astype(bf16)
    pre = dot(normed, inw[...], NN)
    hidden = (pre * (1.0 / (1.0 + jnp.exp(-pre)))).astype(bf16)
    out[...] = (mixed + dot(hidden, outw[...], NN)).astype(bf16)


def solution(mesh):
    zs, gs = mesh.shape["space"] // 4, mesh.shape["kgrp"]

    def local(features, positions, wave_index, wave_filter, mix_pair, msg_weight, chan_width, pair_dist,
              neighbours, norm_gain, in_weight, out_weight):
        atoms = features.shape[0]
        dom = gs * atoms
        kw = wave_index.shape[0]
        f32, bf16 = jnp.float32, jnp.bfloat16
        blk = (3, 8, F)
        big = max(kw, dom)
        vm = pltpu.VMEM
        dma = pltpu.SemaphoreType.DMA
        scratch = [
            vm((gs, atoms, F), bf16),
            vm((2, atoms // 4, F), bf16),
            vm((big, big), f32),
            vm((4, 2, kw // 4, dom), bf16),
            vm((dom, 2 * kw), bf16),
            vm((zs, *blk), f32),
            vm(blk, f32),
            vm((3, zs, *blk), bf16),
            vm((3, zs, *blk), bf16),
            vm((zs, *blk), bf16),
            vm((zs, *blk), bf16),
            vm(blk, bf16),
            vm((4, zs, *blk), bf16),
            vm((2 * kw, F), bf16),
            vm((gs, atoms, F), bf16),
            vm((gs, atoms, F), bf16),
            vm((atoms, F), f32),
            vm((atoms, F), bf16),
            vm((3, dom), f32),
            vm((3, kw), jnp.int32),
            vm((2 * WB, F), f32),
            vm(mix_pair.shape, bf16),
            vm(msg_weight.shape, bf16),
            vm((1, F), f32),
            vm(pair_dist.shape[::-1], f32),
            vm(neighbours.shape[::-1], jnp.int32),
            vm((1, F), f32),
            vm(in_weight.shape, bf16),
            vm(out_weight.shape, bf16),
            pltpu.SemaphoreType.REGULAR((3,)),
            dma((12,)),
            dma, dma, dma, dma,
            dma, dma((2,)),
            dma, dma, dma, dma((4,)),
            dma, dma, dma, dma,
        ]
        return pl.pallas_call(
            functools.partial(kernel, zs, gs),
            out_shape=jax.ShapeDtypeStruct((atoms, F), bf16),
            in_specs=[pl.BlockSpec(memory_space=pl.ANY)] * 12,
            out_specs=pl.BlockSpec(memory_space=pltpu.VMEM),
            scratch_shapes=scratch,
            compiler_params=pltpu.CompilerParams(
                collective_id=0, has_side_effects=True, vmem_limit_bytes=60 * 1024 * 1024
            ),
        )(
            features, positions.T, wave_index.T, wave_filter, mix_pair, msg_weight,
            chan_width.reshape(1, F), pair_dist.T, neighbours.T, norm_gain.reshape(1, F), in_weight, out_weight,
        )

    placed = (
        P(("space", "kgrp"), None), P("space", None), P("kgrp", None), P("kgrp", None), P(), P(), P(),
        P(("space", "kgrp"), None), P(("space", "kgrp"), None), P(), P(), P(),
    )
    return jax.shard_map(
        local, mesh=mesh, in_specs=placed, out_specs=P(("space", "kgrp"), None), check_vma=False
    )
```

```python
import functools
import math

import jax
import jax.numpy as jnp
import numpy as np
from jax import lax
from jax.experimental import pallas as pl
from jax.experimental.pallas import tpu as pltpu
from jax.sharding import PartitionSpec as P

MESH = pl.DeviceIdType.MESH
BOX = 16.0
SLAB_STEP = 0.125
F = 128
WB = 12
TN = (((0,), (0,)), ((), ()))
NN = (((1,), (0,)), ((), ()))

def fit_poly():
    r = 0.5 * np.cos(np.pi * (np.arange(4001) + 0.5) / 4001 / 2)
    t = r * r
    cheb = np.polynomial.chebyshev
    sin_p = cheb.Chebyshev.fit(t, math.sqrt(2) * np.sin(np.pi * r) / r, 4, domain=[0.0, 0.25])
    cos_p = cheb.Chebyshev.fit(t, math.sqrt(2) * np.cos(np.pi * r), 4, domain=[0.0, 0.25])
    to = lambda p: tuple(float(v) for v in p.convert(kind=np.polynomial.Polynomial).coef)
    return to(sin_p), to(cos_p)


SIN_C, COS_C = fit_poly()


def cos_sin_turns(u):
    r = u - jnp.round(u)
    t = r * r
    s = t * SIN_C[-1] + SIN_C[-2]
    for coef in SIN_C[-3::-1]:
        s = s * t + coef
    s = s * r
    c = t * COS_C[-1] + COS_C[-2]
    for coef in COS_C[-3::-1]:
        c = c * t + coef
    return 1.0 - s * s, s * c


def split3(v):
    hi = v.astype(jnp.bfloat16).astype(jnp.float32)
    mid = (v - hi).astype(jnp.bfloat16).astype(jnp.float32)
    return jnp.concatenate([hi, mid, v - hi - mid], axis=0).astype(jnp.bfloat16)


def low_rows(shape):
    return lax.broadcasted_iota(jnp.int32, shape, len(shape) - 2) < 4


def to_blocks(re, im):
    pairs = re.shape[0] // (2 * WB)
    a = re.reshape(pairs, 3, 8, F)
    b = im.reshape(pairs, 3, 8, F)
    a0, a1, a2 = a[:, 0], a[:, 1], a[:, 2]
    b0, b1, b2 = b[:, 0], b[:, 1], b[:, 2]
    low = low_rows(a1.shape)
    x = jnp.where(low, a1, pltpu.roll(b1, 4, 1))
    y = jnp.where(low, pltpu.roll(a1, 4, 1), b1)
    first = jnp.stack([a0, b0, x], axis=1)
    second = jnp.stack([a2, b2, y], axis=1)
    return jnp.stack([first, second], axis=1).reshape(2 * pairs, 3, 8, F)


def from_blocks(v):
    pairs = v.shape[0] // 2
    v = v.reshape(pairs, 2, 3, 8, F)
    x, y = v[:, 0, 2], v[:, 1, 2]
    low = low_rows(x.shape)
    a1 = jnp.where(low, x, pltpu.roll(y, 4, 1))
    b1 = jnp.where(low, pltpu.roll(x, 4, 1), y)
    re = jnp.stack([v[:, 0, 0], a1, v[:, 1, 0]], axis=1).reshape(pairs * 24, F)
    im = jnp.stack([v[:, 0, 1], b1, v[:, 1, 1]], axis=1).reshape(pairs * 24, F)
    return re, im


def far_first(n):
    return sorted(range(1, n), key=lambda o: -min(o, n - o))


def group_order(n):
    nx = min(4, n)
    hops = lambda j: 2 * (j // nx) + min(j % nx, nx - j % nx)
    back = [j // nx * nx + (nx - j % nx) % nx for j in range(n)]
    return nx, sorted(range(1, n), key=lambda j: -hops(j)), back


def slot_of(o, n):
    return 0 if o == 0 else 2 * o - 1 if o <= n // 2 else 2 * (n - o)


def kernel(
    zs, gs, feat_h, pos_h, wave_h, filt_h, mix_h, msgw_h, width_h, dist_h, nbr_h, gain_h, inw_h, outw_h, out,
    fall, halo, ut, pt, pcs, stage, acc, sc_buf, rc_buf, sy_buf, ry_buf, sz_buf, rz_buf,
    ysrc, yall, yv, es, er, msg_t, feat, pos, wave, filt, mix, msgw, width, dist, nbr, gain, inw, outw,
    know, in_s, ag_s, ag_r, ha_s, ha_r, c_s, c_r, y_s, y_r, z_s, z_r, zb_s, zb_r, yb_s, yb_r, e_s, e_r,
):
    f32, bf16 = jnp.float32, jnp.bfloat16
    dot = functools.partial(lax.dot_general, preferred_element_type=f32)
    me_s, me_g = lax.axis_index("space"), lax.axis_index("kgrp")
    z, yl, c = me_s // 4, lax.rem(me_s // 2, 2), lax.rem(me_s, 2)
    n_dev = 4 * zs * gs
    flat = me_s * gs + me_g
    up, down = lax.rem(flat + 1, n_dev), lax.rem(flat + n_dev - 1, n_dev)
    up = (up // gs, lax.rem(up, gs))
    down = (down // gs, lax.rem(down, gs))
    nx, group_far, group_back = group_order(gs)
    row, col = me_g // nx, lax.rem(me_g, nx)
    group = [(me_s, lax.rem(row + j // nx, gs // nx) * nx + lax.rem(col + j % nx, nx)) for j in range(gs)]
    core = (z * 4 + yl * 2 + 1 - c, me_g)
    ypeer = (z * 4 + (1 - yl) * 2 + c, me_g)
    diagonal = (z * 4 + (1 - yl) * 2 + 1 - c, me_g)
    ring_z = [lax.rem(z + o, zs) for o in range(zs)]
    ring = [(at * 4 + yl * 2 + c, me_g) for at in ring_z]
    offset_of = sorted(range(zs), key=lambda o: slot_of(o, zs))
    atoms = feat.shape[0]
    kw = wave.shape[1]
    rows = kw // 4

    def remote(src, dst, send, recv, device):
        return pltpu.make_async_remote_copy(
            src_ref=src, dst_ref=dst, send_sem=send, recv_sem=recv, device_id=device, device_id_type=MESH
        )

    def signal(sem, device):
        pl.semaphore_signal(sem, inc=1, device_id=device, device_id_type=MESH)

    barrier = pltpu.get_barrier_semaphore()
    peers = group[1:] + [up, down, core, ypeer, diagonal, ring[1], ring[zs - 1]]
    for device in peers:
        signal(barrier, device)

    pair = ((c * 2 + yl) * zs + z) // 2
    filt_part = filt_h.at[pl.ds(pl.multiple_of(pair * 24, 8), 24)]
    fetch = [
        pltpu.make_async_copy(src, dst, in_s.at[i])
        for i, (src, dst) in enumerate(
            (
                (pos_h, pos), (wave_h, wave), (feat_h, feat), (filt_part, filt), (mix_h, mix), (msgw_h, msgw),
                (width_h, width), (dist_h, dist), (nbr_h, nbr), (gain_h, gain), (inw_h, inw), (outw_h, outw),
            )
        )
    ]
    for copy in fetch:
        copy.start()
    fetch[0].wait()
    fetch[1].wait()

    turned = [pos[:, pl.ds(pl.multiple_of(at * atoms, atoms), atoms)] for _, at in group]
    scales = lax.broadcasted_iota(jnp.int32, pos.shape, 0)
    scales = jnp.where(scales < 2, 1.0 / BOX, 1.0 / (n_dev * atoms * SLAB_STEP)).astype(f32)
    pieces = split3(jnp.concatenate(turned, axis=1) * scales)
    counts = wave[...].astype(f32)
    counts = jnp.concatenate([counts, counts, counts], axis=0).astype(bf16)

    fetch[2].wait()
    pl.semaphore_wait(barrier, len(peers))

    for j in group_far:
        remote(feat, fall.at[group_back[j]], ag_s, ag_r, group[j]).start()
    edge = atoms // 4
    remote(feat.at[pl.ds(atoms - edge, edge)], halo.at[0], ha_s, ha_r, up).start()
    remote(feat.at[pl.ds(0, edge)], halo.at[1], ha_s, ha_r, down).start()
    fall[0] = feat[...]

    def received(ref, sem):
        remote(ref, ref, ag_s, sem, core).wait_recv()

    def sent(ref, sem):
        remote(ref, ref, sem, ag_r, core).wait_send()

    steps = []
    reach = 1
    while reach < zs // 2:
        steps.append(reach)
        reach *= 2

    def tell(i):
        if i < len(steps):
            signal(know.at[i], ring[steps[i]])
            signal(know.at[i], ring[zs - steps[i]])

    def hear(i):
        if i < len(steps):
            pl.semaphore_wait(know.at[i], 2)

    tell(0)

    chunk = 16 if rows % 16 == 0 else 8
    dom = gs * atoms
    ut[0:kw, 0:dom] = dot(counts, pieces, TN)

    @pl.loop(0, kw // chunk)
    def _(i):
        at = pl.ds(pl.multiple_of(i * chunk, chunk), chunk)
        cos_v, sin_v = cos_sin_turns(ut[at, 0:dom])
        quarter = i // (rows // chunk)
        at = pl.ds(pl.multiple_of(lax.rem(i, rows // chunk) * chunk, chunk), chunk)
        pt[quarter, 0, at, :] = cos_v.astype(bf16)
        pt[quarter, 1, at, :] = sin_v.astype(bf16)

    hear(0)
    tell(1)
    hear(1)
    tell(2)
    if gs > 1:
        received(fall.at[pl.ds(1, gs - 1)], ag_r)

    feats = fall[...].reshape(gs * atoms, F)

    def structure(core_at, y_at):
        sums = dot(pt[core_at * 2 + y_at].reshape(2 * rows, dom), feats, NN)
        stage[...] = to_blocks(sums[:rows], sums[rows:])
        return [stage[pl.ds(ring_z[o], 1)][0] for o in offset_of]

    def to_core(i, y_at):
        for s, v in enumerate(structure(1 - c, y_at)):
            sc_buf[i, s] = v.astype(bf16)
        remote(sc_buf.at[i], rc_buf.at[i], c_s, c_r.at[i], core).start()

    to_core(0, 1 - yl)
    mine = structure(c, 1 - yl)
    for s in range(zs):
        acc[s] = mine[s]
    to_core(1, yl)
    parts = ((12, 16), (6, 12), (0, 6)) if zs == 16 else ((zs // 2, zs), (0, zs // 2))
    received(rc_buf.at[0], c_r.at[0])
    for i, (lo, hi) in enumerate(parts):
        for s in range(lo, hi):
            sy_buf[s] = (acc[s] + rc_buf[0, s].astype(f32)).astype(bf16)
        part = pl.ds(lo, hi - lo)
        remote(sy_buf.at[part], ry_buf.at[part], y_s, y_r.at[i], ypeer).start()
    mine = structure(c, yl)
    received(rc_buf.at[1], c_r.at[1])
    for s in range(zs):
        acc[s] = mine[s] + rc_buf[1, s].astype(f32)
    hear(2)
    for i, (lo, hi) in enumerate(parts):
        received(ry_buf.at[pl.ds(lo, hi - lo)], y_r.at[i])
        for s in range(hi - 1, lo - 1, -1):
            total = acc[s] + ry_buf[s].astype(f32)
            if s == 0:
                acc[0] = total
                continue
            sz_buf[s] = total.astype(bf16)
            o = offset_of[s]
            remote(sz_buf.at[s], rz_buf.at[slot_of(zs - o, zs)], z_s, z_r, ring[o]).start()

    for copy in fetch[3:]:
        copy.wait()
    total = acc[0]
    others = pl.ds(1, zs - 1)
    received(rz_buf.at[others], z_r)
    for s in range(1, zs):
        total = total + rz_buf[s].astype(f32)

    a = (total * (1.0 / math.sqrt(n_dev * atoms))).reshape(24, F).astype(bf16)
    r0 = dot(a, mix[0], NN).reshape(3, 8, F)
    r1 = dot(a, mix[1], NN).reshape(3, 8, F)
    odd = lax.rem(z, 2) == 1
    fil = filt[...].reshape(3, 8, F)
    low = low_rows((8, F))
    swapped = pltpu.roll(fil[1], 4, 0)
    f_main = jnp.where(odd, fil[2], fil[0])
    f_mixed = jnp.where(jnp.logical_xor(low, odd), fil[1], swapped)
    r1_swapped = pltpu.roll(r1[2], 4, 0)
    y_val = jnp.stack(
        [
            f_main * (r0[0] - r1[1]),
            f_main * (r1[0] + r0[1]),
            f_mixed * jnp.where(low, r0[2] - r1_swapped, r0[2] + r1_swapped),
        ],
        axis=0,
    ).astype(bf16)
    ysrc[...] = y_val
    here = c * 2 + yl
    cuts = (0, 5, 9, 13, 15, 16) if zs == 16 else (0, zs // 2, zs)
    for o in far_first(zs):
        s = slot_of(zs - o, zs)
        part = sum(s >= hi for hi in cuts[1:])
        remote(ysrc, yall.at[here, s], zb_s, zb_r.at[part], ring[o]).start()
    yall[pl.ds(here, 1), 0] = y_val[None]

    send_order = group_far + [0]
    lanes = [pieces[:, j * atoms : (j + 1) * atoms] for j in send_order]
    ut[0:dom, 0:kw] = dot(jnp.concatenate(lanes, axis=1), counts, TN)

    @pl.loop(0, dom // 16)
    def _(i):
        at = pl.ds(pl.multiple_of(i * 16, 16), 16)
        cos_v, sin_v = cos_sin_turns(ut[at, 0:kw])
        pcs[at, 0:kw] = cos_v.astype(bf16)
        pcs[at, kw : 2 * kw] = sin_v.astype(bf16)

    received(halo, ha_r)
    weight = msgw[...]
    ext = jnp.concatenate(
        [
            dot(halo[0], weight, NN),
            dot(feat[...], weight, NN),
            dot(halo[1], weight, NN),
            jnp.zeros((edge * 2, F), f32),
        ],
        axis=0,
    )
    ext_t = ext.T.astype(bf16)
    inv_width = (1.0 / jnp.broadcast_to(width[...], (F, F))).T
    row_ids = lax.broadcasted_iota(jnp.int32, (2 * atoms, atoms), 0)
    message = jnp.zeros((F, atoms), f32)
    for j in range(nbr.shape[0]):
        hot = jnp.where(row_ids == nbr[j : j + 1, :], 1.0, 0.0).astype(bf16)
        near = dot(ext_t, hot, NN)
        message = message + jnp.exp(-(dist[j : j + 1, :] * inv_width)) * near
    msg_t[...] = message.T

    for i in range(len(cuts) - 1):
        lo, hi = cuts[i], cuts[i + 1]
        if hi > max(lo, 1):
            received(yall.at[here, pl.ds(max(lo, 1), hi - max(lo, 1))], zb_r.at[i])
        here_part = yall.at[here, pl.ds(lo, hi - lo)]
        for device in (diagonal, ypeer, core):
            remote(here_part, here_part, yb_s, yb_r, device).start()
    received(yall.at[pl.ds(1, 3)], yb_r)

    slots = []
    for t in range(zs):
        o = lax.rem(t - z + zs, zs)
        slots.append(jnp.where(o <= zs // 2, jnp.maximum(2 * o - 1, 0), 2 * (zs - o)))
    for q in range(4):
        blocks = [yall[q, pl.ds(slots[t], 1)] for t in range(zs)]
        re, im = from_blocks(jnp.concatenate(blocks, axis=0).astype(f32))
        yv[q * rows : (q + 1) * rows, :] = re.astype(bf16)
        yv[kw + q * rows : kw + (q + 1) * rows, :] = im.astype(bf16)
    inv_scale = 1.0 / math.sqrt(kw * gs)

    bounds = (0, 1, 4, 8) if gs == 8 else (0, gs)
    for lo, hi in zip(bounds[:-1], bounds[1:]):
        terms = dot(pcs[lo * atoms : hi * atoms, :], yv[...], NN) * inv_scale
        for i in range(lo, hi):
            j = send_order[i]
            term = terms[(i - lo) * atoms : (i - lo + 1) * atoms]
            if j == 0:
                ewald = term
                continue
            es[j] = term.astype(bf16)
            remote(es.at[j], er.at[group_back[j]], e_s, e_r, group[j]).start()

    sent(halo, ha_s)
    sent(sc_buf, c_s)
    sent(sy_buf, y_s)
    sent(sz_buf.at[others], z_s)
    sent(yall.at[here, others], zb_s)
    sent(yall.at[pl.ds(1, 3)], yb_s)
    if gs > 1:
        rest = pl.ds(1, gs - 1)
        sent(fall.at[rest], ag_s)
        received(er.at[rest], e_r)
        sent(es.at[rest], e_s)
    for o in range(1, gs):
        ewald = ewald + er[o].astype(f32)

    mixed = feat[...].astype(f32) + msg_t[...] + ewald
    inverse = lax.rsqrt(jnp.mean(mixed * mixed, axis=1, keepdims=True) + 1e-06)
    normed = (mixed * inverse * gain[...]).astype(bf16)
    pre = dot(normed, inw[...], NN)
    hidden = (pre * (1.0 / (1.0 + jnp.exp(-pre)))).astype(bf16)
    out[...] = (mixed + dot(hidden, outw[...], NN)).astype(bf16)


def solution(mesh):
    zs, gs = mesh.shape["space"] // 4, mesh.shape["kgrp"]

    def local(features, positions, wave_index, wave_filter, mix_pair, msg_weight, chan_width, pair_dist,
              neighbours, norm_gain, in_weight, out_weight):
        atoms = features.shape[0]
        dom = gs * atoms
        kw = wave_index.shape[0]
        f32, bf16 = jnp.float32, jnp.bfloat16
        blk = (3, 8, F)
        big = max(kw, dom)
        vm = pltpu.VMEM
        dma = pltpu.SemaphoreType.DMA
        scratch = [
            vm((gs, atoms, F), bf16),
            vm((2, atoms // 4, F), bf16),
            vm((big, big), f32),
            vm((4, 2, kw // 4, dom), bf16),
            vm((dom, 2 * kw), bf16),
            vm((zs, *blk), f32),
            vm((zs, *blk), f32),
            vm((2, zs, *blk), bf16),
            vm((2, zs, *blk), bf16),
            vm((zs, *blk), bf16),
            vm((zs, *blk), bf16),
            vm((zs, *blk), bf16),
            vm((zs, *blk), bf16),
            vm(blk, bf16),
            vm((4, zs, *blk), bf16),
            vm((2 * kw, F), bf16),
            vm((gs, atoms, F), bf16),
            vm((gs, atoms, F), bf16),
            vm((atoms, F), f32),
            vm((atoms, F), bf16),
            vm((3, dom), f32),
            vm((3, kw), jnp.int32),
            vm((2 * WB, F), f32),
            vm(mix_pair.shape, bf16),
            vm(msg_weight.shape, bf16),
            vm((1, F), f32),
            vm(pair_dist.shape[::-1], f32),
            vm(neighbours.shape[::-1], jnp.int32),
            vm((1, F), f32),
            vm(in_weight.shape, bf16),
            vm(out_weight.shape, bf16),
            pltpu.SemaphoreType.REGULAR((3,)),
            dma((12,)),
            dma, dma, dma, dma,
            dma, dma((2,)), dma, dma((3,)),
            dma, dma, dma, dma((5,)),
            dma, dma, dma, dma,
        ]
        return pl.pallas_call(
            functools.partial(kernel, zs, gs),
            out_shape=jax.ShapeDtypeStruct((atoms, F), bf16),
            in_specs=[pl.BlockSpec(memory_space=pl.ANY)] * 12,
            out_specs=pl.BlockSpec(memory_space=pltpu.VMEM),
            scratch_shapes=scratch,
            compiler_params=pltpu.CompilerParams(
                collective_id=0, has_side_effects=True, vmem_limit_bytes=60 * 1024 * 1024
            ),
        )(
            features, positions.T, wave_index.T, wave_filter, mix_pair, msg_weight,
            chan_width.reshape(1, F), pair_dist.T, neighbours.T, norm_gain.reshape(1, F), in_weight, out_weight,
        )

    placed = (
        P(("space", "kgrp"), None), P("space", None), P("kgrp", None), P("kgrp", None), P(), P(), P(),
        P(("space", "kgrp"), None), P(("space", "kgrp"), None), P(), P(), P(),
    )
    return jax.shard_map(
        local, mesh=mesh, in_specs=placed, out_specs=P(("space", "kgrp"), None), check_vma=False
    )
```

```python
import functools
import math

import jax
import jax.numpy as jnp
import numpy as np
from jax import lax
from jax.experimental import pallas as pl
from jax.experimental.pallas import tpu as pltpu
from jax.sharding import PartitionSpec as P

MESH = pl.DeviceIdType.MESH
BOX = 16.0
SLAB_STEP = 0.125
F = 128
WB = 12
TN = (((0,), (0,)), ((), ()))
NN = (((1,), (0,)), ((), ()))

def fit_poly():
    r = 0.5 * np.cos(np.pi * (np.arange(4001) + 0.5) / 4001 / 2)
    t = r * r
    cheb = np.polynomial.chebyshev
    sin_p = cheb.Chebyshev.fit(t, math.sqrt(2) * np.sin(np.pi * r) / r, 4, domain=[0.0, 0.25])
    cos_p = cheb.Chebyshev.fit(t, math.sqrt(2) * np.cos(np.pi * r), 4, domain=[0.0, 0.25])
    to = lambda p: tuple(float(v) for v in p.convert(kind=np.polynomial.Polynomial).coef)
    return to(sin_p), to(cos_p)


SIN_C, COS_C = fit_poly()


def cos_sin_turns(u):
    r = u - jnp.round(u)
    t = r * r
    s = t * SIN_C[-1] + SIN_C[-2]
    for coef in SIN_C[-3::-1]:
        s = s * t + coef
    s = s * r
    c = t * COS_C[-1] + COS_C[-2]
    for coef in COS_C[-3::-1]:
        c = c * t + coef
    return 1.0 - s * s, s * c


def split3(v):
    hi = v.astype(jnp.bfloat16).astype(jnp.float32)
    mid = (v - hi).astype(jnp.bfloat16).astype(jnp.float32)
    return jnp.concatenate([hi, mid, v - hi - mid], axis=0).astype(jnp.bfloat16)


def low_rows(shape):
    return lax.broadcasted_iota(jnp.int32, shape, len(shape) - 2) < 4


def to_blocks(re, im):
    pairs = re.shape[0] // (2 * WB)
    a = re.reshape(pairs, 3, 8, F)
    b = im.reshape(pairs, 3, 8, F)
    a0, a1, a2 = a[:, 0], a[:, 1], a[:, 2]
    b0, b1, b2 = b[:, 0], b[:, 1], b[:, 2]
    low = low_rows(a1.shape)
    x = jnp.where(low, a1, pltpu.roll(b1, 4, 1))
    y = jnp.where(low, pltpu.roll(a1, 4, 1), b1)
    first = jnp.stack([a0, b0, x], axis=1)
    second = jnp.stack([a2, b2, y], axis=1)
    return jnp.stack([first, second], axis=1).reshape(2 * pairs, 3, 8, F)


def from_blocks(v):
    pairs = v.shape[0] // 2
    v = v.reshape(pairs, 2, 3, 8, F)
    x, y = v[:, 0, 2], v[:, 1, 2]
    low = low_rows(x.shape)
    a1 = jnp.where(low, x, pltpu.roll(y, 4, 1))
    b1 = jnp.where(low, pltpu.roll(x, 4, 1), y)
    re = jnp.stack([v[:, 0, 0], a1, v[:, 1, 0]], axis=1).reshape(pairs * 24, F)
    im = jnp.stack([v[:, 0, 1], b1, v[:, 1, 1]], axis=1).reshape(pairs * 24, F)
    return re, im


def far_first(n):
    return sorted(range(1, n), key=lambda o: -min(o, n - o))


def group_order(n):
    nx = min(4, n)
    hops = lambda j: 2 * (j // nx) + min(j % nx, nx - j % nx)
    back = [j // nx * nx + (nx - j % nx) % nx for j in range(n)]
    return nx, sorted(range(1, n), key=lambda j: -hops(j)), back


def slot_of(o, n):
    return 0 if o == 0 else 2 * o - 1 if o <= n // 2 else 2 * (n - o)


def kernel(
    zs, gs, feat_h, pos_h, wave_h, filt_h, mix_h, msgw_h, width_h, dist_h, nbr_h, gain_h, inw_h, outw_h, out,
    fall, halo, ut, pt, pcs, stage, acc, sc_buf, rc_buf, sz_buf, rz_buf,
    ysrc, yall, yv, es, er, msg_t, feat, pos, wave, filt, mix, msgw, width, dist, nbr, gain, inw, outw,
    know, in_s, ag_s, ag_r, ha_s, ha_r, c_s, c_r, z_s, z_r, zb_s, zb_r, yb_s, yb_r, e_s, e_r,
):
    f32, bf16 = jnp.float32, jnp.bfloat16
    dot = functools.partial(lax.dot_general, preferred_element_type=f32)
    me_s, me_g = lax.axis_index("space"), lax.axis_index("kgrp")
    z, yl, c = me_s // 4, lax.rem(me_s // 2, 2), lax.rem(me_s, 2)
    n_dev = 4 * zs * gs
    flat = me_s * gs + me_g
    up, down = lax.rem(flat + 1, n_dev), lax.rem(flat + n_dev - 1, n_dev)
    up = (up // gs, lax.rem(up, gs))
    down = (down // gs, lax.rem(down, gs))
    nx, group_far, group_back = group_order(gs)
    row, col = me_g // nx, lax.rem(me_g, nx)
    group = [(me_s, lax.rem(row + j // nx, gs // nx) * nx + lax.rem(col + j % nx, nx)) for j in range(gs)]
    core = (z * 4 + yl * 2 + 1 - c, me_g)
    ypeer = (z * 4 + (1 - yl) * 2 + c, me_g)
    diagonal = (z * 4 + (1 - yl) * 2 + 1 - c, me_g)
    ring_z = [lax.rem(z + o, zs) for o in range(zs)]
    ring = [(at * 4 + yl * 2 + c, me_g) for at in ring_z]
    offset_of = sorted(range(zs), key=lambda o: slot_of(o, zs))
    atoms = feat.shape[0]
    kw = wave.shape[1]
    rows = kw // 4

    def remote(src, dst, send, recv, device):
        return pltpu.make_async_remote_copy(
            src_ref=src, dst_ref=dst, send_sem=send, recv_sem=recv, device_id=device, device_id_type=MESH
        )

    def signal(sem, device):
        pl.semaphore_signal(sem, inc=1, device_id=device, device_id_type=MESH)

    barrier = pltpu.get_barrier_semaphore()
    peers = group[1:] + [up, down, core, ypeer, diagonal, ring[1], ring[zs - 1]]
    for device in peers:
        signal(barrier, device)

    pair = ((c * 2 + yl) * zs + z) // 2
    filt_part = filt_h.at[pl.ds(pl.multiple_of(pair * 24, 8), 24)]
    fetch = [
        pltpu.make_async_copy(src, dst, in_s.at[i])
        for i, (src, dst) in enumerate(
            (
                (pos_h, pos), (wave_h, wave), (feat_h, feat), (filt_part, filt), (mix_h, mix), (msgw_h, msgw),
                (width_h, width), (dist_h, dist), (nbr_h, nbr), (gain_h, gain), (inw_h, inw), (outw_h, outw),
            )
        )
    ]
    for copy in fetch:
        copy.start()
    fetch[0].wait()
    fetch[1].wait()

    turned = [pos[:, pl.ds(pl.multiple_of(at * atoms, atoms), atoms)] for _, at in group]
    scales = lax.broadcasted_iota(jnp.int32, pos.shape, 0)
    scales = jnp.where(scales < 2, 1.0 / BOX, 1.0 / (n_dev * atoms * SLAB_STEP)).astype(f32)
    pieces = split3(jnp.concatenate(turned, axis=1) * scales)
    counts = wave[...].astype(f32)
    counts = jnp.concatenate([counts, counts, counts], axis=0).astype(bf16)

    fetch[2].wait()
    pl.semaphore_wait(barrier, len(peers))

    for j in group_far:
        remote(feat, fall.at[group_back[j]], ag_s, ag_r, group[j]).start()
    edge = atoms // 4
    remote(feat.at[pl.ds(atoms - edge, edge)], halo.at[0], ha_s, ha_r, up).start()
    remote(feat.at[pl.ds(0, edge)], halo.at[1], ha_s, ha_r, down).start()
    fall[0] = feat[...]

    def received(ref, sem):
        remote(ref, ref, ag_s, sem, core).wait_recv()

    def sent(ref, sem):
        remote(ref, ref, sem, ag_r, core).wait_send()

    steps = []
    reach = 1
    while reach < zs // 2:
        steps.append(reach)
        reach *= 2

    def tell(i):
        if i < len(steps):
            signal(know.at[i], ring[steps[i]])
            signal(know.at[i], ring[zs - steps[i]])

    def hear(i):
        if i < len(steps):
            pl.semaphore_wait(know.at[i], 2)

    tell(0)

    chunk = 16 if rows % 16 == 0 else 8
    dom = gs * atoms
    ut[0:kw, 0:dom] = dot(counts, pieces, TN)

    @pl.loop(0, kw // chunk)
    def _(i):
        at = pl.ds(pl.multiple_of(i * chunk, chunk), chunk)
        cos_v, sin_v = cos_sin_turns(ut[at, 0:dom])
        quarter = i // (rows // chunk)
        at = pl.ds(pl.multiple_of(lax.rem(i, rows // chunk) * chunk, chunk), chunk)
        pt[quarter, 0, at, :] = cos_v.astype(bf16)
        pt[quarter, 1, at, :] = sin_v.astype(bf16)

    hear(0)
    tell(1)
    hear(1)
    tell(2)
    if gs > 1:
        received(fall.at[pl.ds(1, gs - 1)], ag_r)

    feats = fall[...].reshape(gs * atoms, F)

    def structure(core_at, y_at):
        sums = dot(pt[core_at * 2 + y_at].reshape(2 * rows, dom), feats, NN)
        stage[...] = to_blocks(sums[:rows], sums[rows:])
        return [stage[pl.ds(ring_z[o], 1)][0] for o in offset_of]

    cut = zs // 2
    parts = ((cut, zs), (0, cut))
    quad = (diagonal, ypeer, core)

    def swap(k, i):
        part = pl.ds(parts[i][0], parts[i][1] - parts[i][0])
        remote(sc_buf.at[k, part], rc_buf.at[k, part], c_s, c_r.at[i], quad[k]).start()

    for k, (core_at, y_at) in enumerate(((1 - c, 1 - yl), (c, 1 - yl), (1 - c, yl))):
        for s, v in enumerate(structure(core_at, y_at)):
            sc_buf[k, s] = v.astype(bf16)
        swap(k, 0)
        swap(k, 1)
    mine = structure(c, yl)
    hear(2)
    for i, (lo, hi) in enumerate(parts):
        received(rc_buf.at[:, pl.ds(lo, hi - lo)], c_r.at[i])
        for s in range(hi - 1, lo - 1, -1):
            total = mine[s]
            for k in range(3):
                total = total + rc_buf[k, s].astype(f32)
            if s == 0:
                acc[...] = total
                continue
            sz_buf[s] = total.astype(bf16)
            o = offset_of[s]
            remote(sz_buf.at[s], rz_buf.at[slot_of(zs - o, zs)], z_s, z_r, ring[o]).start()

    for copy in fetch[3:]:
        copy.wait()
    total = acc[...]
    others = pl.ds(1, zs - 1)
    received(rz_buf.at[others], z_r)
    for s in range(1, zs):
        total = total + rz_buf[s].astype(f32)

    a = (total * (1.0 / math.sqrt(n_dev * atoms))).reshape(24, F).astype(bf16)
    r0 = dot(a, mix[0], NN).reshape(3, 8, F)
    r1 = dot(a, mix[1], NN).reshape(3, 8, F)
    odd = lax.rem(z, 2) == 1
    fil = filt[...].reshape(3, 8, F)
    low = low_rows((8, F))
    swapped = pltpu.roll(fil[1], 4, 0)
    f_main = jnp.where(odd, fil[2], fil[0])
    f_mixed = jnp.where(jnp.logical_xor(low, odd), fil[1], swapped)
    r1_swapped = pltpu.roll(r1[2], 4, 0)
    y_val = jnp.stack(
        [
            f_main * (r0[0] - r1[1]),
            f_main * (r1[0] + r0[1]),
            f_mixed * jnp.where(low, r0[2] - r1_swapped, r0[2] + r1_swapped),
        ],
        axis=0,
    ).astype(bf16)
    ysrc[...] = y_val
    here = c * 2 + yl
    cuts = (0, 5, 9, 13, 16) if zs == 16 else (0, zs // 2, zs)
    for o in far_first(zs):
        s = slot_of(zs - o, zs)
        part = sum(s >= hi for hi in cuts[1:])
        remote(ysrc, yall.at[here, s], zb_s, zb_r.at[part], ring[o]).start()
    yall[pl.ds(here, 1), 0] = y_val[None]

    send_order = group_far + [0]
    lanes = [pieces[:, j * atoms : (j + 1) * atoms] for j in send_order]
    ut[0:dom, 0:kw] = dot(jnp.concatenate(lanes, axis=1), counts, TN)

    @pl.loop(0, dom // 16)
    def _(i):
        at = pl.ds(pl.multiple_of(i * 16, 16), 16)
        cos_v, sin_v = cos_sin_turns(ut[at, 0:kw])
        pcs[at, 0:kw] = cos_v.astype(bf16)
        pcs[at, kw : 2 * kw] = sin_v.astype(bf16)

    received(halo, ha_r)
    weight = msgw[...]
    ext = jnp.concatenate(
        [
            dot(halo[0], weight, NN),
            dot(feat[...], weight, NN),
            dot(halo[1], weight, NN),
            jnp.zeros((edge * 2, F), f32),
        ],
        axis=0,
    )
    ext_t = ext.T.astype(bf16)
    inv_width = (1.0 / jnp.broadcast_to(width[...], (F, F))).T
    row_ids = lax.broadcasted_iota(jnp.int32, (2 * atoms, atoms), 0)
    message = jnp.zeros((F, atoms), f32)
    for j in range(nbr.shape[0]):
        hot = jnp.where(row_ids == nbr[j : j + 1, :], 1.0, 0.0).astype(bf16)
        near = dot(ext_t, hot, NN)
        message = message + jnp.exp(-(dist[j : j + 1, :] * inv_width)) * near
    msg_t[...] = message.T

    for i in range(len(cuts) - 1):
        lo, hi = cuts[i], cuts[i + 1]
        if hi > max(lo, 1):
            received(yall.at[here, pl.ds(max(lo, 1), hi - max(lo, 1))], zb_r.at[i])
        here_part = yall.at[here, pl.ds(lo, hi - lo)]
        for device in (diagonal, ypeer, core):
            remote(here_part, here_part, yb_s, yb_r, device).start()
    received(yall.at[pl.ds(1, 3)], yb_r)

    slots = []
    for t in range(zs):
        o = lax.rem(t - z + zs, zs)
        slots.append(jnp.where(o <= zs // 2, jnp.maximum(2 * o - 1, 0), 2 * (zs - o)))
    for q in range(4):
        blocks = [yall[q, pl.ds(slots[t], 1)] for t in range(zs)]
        re, im = from_blocks(jnp.concatenate(blocks, axis=0).astype(f32))
        yv[q * rows : (q + 1) * rows, :] = re.astype(bf16)
        yv[kw + q * rows : kw + (q + 1) * rows, :] = im.astype(bf16)
    inv_scale = 1.0 / math.sqrt(kw * gs)

    bounds = (0, 1, 4, 8) if gs == 8 else (0, gs)
    for lo, hi in zip(bounds[:-1], bounds[1:]):
        terms = dot(pcs[lo * atoms : hi * atoms, :], yv[...], NN) * inv_scale
        for i in range(lo, hi):
            j = send_order[i]
            term = terms[(i - lo) * atoms : (i - lo + 1) * atoms]
            if j == 0:
                ewald = term
                continue
            es[j] = term.astype(bf16)
            remote(es.at[j], er.at[group_back[j]], e_s, e_r, group[j]).start()

    sent(halo, ha_s)
    sent(sc_buf, c_s)
    sent(sz_buf.at[others], z_s)
    sent(yall.at[here, others], zb_s)
    sent(yall.at[pl.ds(1, 3)], yb_s)
    if gs > 1:
        rest = pl.ds(1, gs - 1)
        sent(fall.at[rest], ag_s)
        received(er.at[rest], e_r)
        sent(es.at[rest], e_s)
    for o in range(1, gs):
        ewald = ewald + er[o].astype(f32)

    mixed = feat[...].astype(f32) + msg_t[...] + ewald
    inverse = lax.rsqrt(jnp.mean(mixed * mixed, axis=1, keepdims=True) + 1e-06)
    normed = (mixed * inverse * gain[...]).astype(bf16)
    pre = dot(normed, inw[...], NN)
    hidden = (pre * (1.0 / (1.0 + jnp.exp(-pre)))).astype(bf16)
    out[...] = (mixed + dot(hidden, outw[...], NN)).astype(bf16)


def solution(mesh):
    zs, gs = mesh.shape["space"] // 4, mesh.shape["kgrp"]

    def local(features, positions, wave_index, wave_filter, mix_pair, msg_weight, chan_width, pair_dist,
              neighbours, norm_gain, in_weight, out_weight):
        atoms = features.shape[0]
        dom = gs * atoms
        kw = wave_index.shape[0]
        f32, bf16 = jnp.float32, jnp.bfloat16
        blk = (3, 8, F)
        big = max(kw, dom)
        vm = pltpu.VMEM
        dma = pltpu.SemaphoreType.DMA
        scratch = [
            vm((gs, atoms, F), bf16),
            vm((2, atoms // 4, F), bf16),
            vm((big, big), f32),
            vm((4, 2, kw // 4, dom), bf16),
            vm((dom, 2 * kw), bf16),
            vm((zs, *blk), f32),
            vm(blk, f32),
            vm((3, zs, *blk), bf16),
            vm((3, zs, *blk), bf16),
            vm((zs, *blk), bf16),
            vm((zs, *blk), bf16),
            vm(blk, bf16),
            vm((4, zs, *blk), bf16),
            vm((2 * kw, F), bf16),
            vm((gs, atoms, F), bf16),
            vm((gs, atoms, F), bf16),
            vm((atoms, F), f32),
            vm((atoms, F), bf16),
            vm((3, dom), f32),
            vm((3, kw), jnp.int32),
            vm((2 * WB, F), f32),
            vm(mix_pair.shape, bf16),
            vm(msg_weight.shape, bf16),
            vm((1, F), f32),
            vm(pair_dist.shape[::-1], f32),
            vm(neighbours.shape[::-1], jnp.int32),
            vm((1, F), f32),
            vm(in_weight.shape, bf16),
            vm(out_weight.shape, bf16),
            pltpu.SemaphoreType.REGULAR((3,)),
            dma((12,)),
            dma, dma, dma, dma,
            dma, dma((2,)),
            dma, dma, dma, dma((4,)),
            dma, dma, dma, dma,
        ]
        return pl.pallas_call(
            functools.partial(kernel, zs, gs),
            out_shape=jax.ShapeDtypeStruct((atoms, F), bf16),
            in_specs=[pl.BlockSpec(memory_space=pl.ANY)] * 12,
            out_specs=pl.BlockSpec(memory_space=pltpu.VMEM),
            scratch_shapes=scratch,
            compiler_params=pltpu.CompilerParams(
                collective_id=0, has_side_effects=True, vmem_limit_bytes=60 * 1024 * 1024
            ),
        )(
            features, positions.T, wave_index.T, wave_filter, mix_pair, msg_weight,
            chan_width.reshape(1, F), pair_dist.T, neighbours.T, norm_gain.reshape(1, F), in_weight, out_weight,
        )

    placed = (
        P(("space", "kgrp"), None), P("space", None), P("kgrp", None), P("kgrp", None), P(), P(), P(),
        P(("space", "kgrp"), None), P(("space", "kgrp"), None), P(), P(), P(),
    )
    return jax.shard_map(
        local, mesh=mesh, in_specs=placed, out_specs=P(("space", "kgrp"), None), check_vma=False
    )
```

```python
import functools
import math

import jax
import jax.numpy as jnp
import numpy as np
from jax import lax
from jax.experimental import pallas as pl
from jax.experimental.pallas import tpu as pltpu
from jax.sharding import PartitionSpec as P

MESH = pl.DeviceIdType.MESH
BOX = 16.0
SLAB_STEP = 0.125
F = 128
WB = 12
TN = (((0,), (0,)), ((), ()))
NN = (((1,), (0,)), ((), ()))

def fit_poly():
    r = 0.5 * np.cos(np.pi * (np.arange(4001) + 0.5) / 4001 / 2)
    t = r * r
    cheb = np.polynomial.chebyshev
    sin_p = cheb.Chebyshev.fit(t, math.sqrt(2) * np.sin(np.pi * r) / r, 4, domain=[0.0, 0.25])
    cos_p = cheb.Chebyshev.fit(t, math.sqrt(2) * np.cos(np.pi * r), 4, domain=[0.0, 0.25])
    to = lambda p: tuple(float(v) for v in p.convert(kind=np.polynomial.Polynomial).coef)
    return to(sin_p), to(cos_p)


SIN_C, COS_C = fit_poly()


def cos_sin_turns(u):
    r = u - jnp.round(u)
    t = r * r
    s = t * SIN_C[-1] + SIN_C[-2]
    for coef in SIN_C[-3::-1]:
        s = s * t + coef
    s = s * r
    c = t * COS_C[-1] + COS_C[-2]
    for coef in COS_C[-3::-1]:
        c = c * t + coef
    return 1.0 - s * s, s * c


def split3(v):
    hi = v.astype(jnp.bfloat16).astype(jnp.float32)
    mid = (v - hi).astype(jnp.bfloat16).astype(jnp.float32)
    return jnp.concatenate([hi, mid, v - hi - mid], axis=0).astype(jnp.bfloat16)


def low_rows(shape):
    return lax.broadcasted_iota(jnp.int32, shape, len(shape) - 2) < 4


def to_blocks(re, im):
    pairs = re.shape[0] // (2 * WB)
    a = re.reshape(pairs, 3, 8, F)
    b = im.reshape(pairs, 3, 8, F)
    a0, a1, a2 = a[:, 0], a[:, 1], a[:, 2]
    b0, b1, b2 = b[:, 0], b[:, 1], b[:, 2]
    low = low_rows(a1.shape)
    x = jnp.where(low, a1, pltpu.roll(b1, 4, 1))
    y = jnp.where(low, pltpu.roll(a1, 4, 1), b1)
    first = jnp.stack([a0, b0, x], axis=1)
    second = jnp.stack([a2, b2, y], axis=1)
    return jnp.stack([first, second], axis=1).reshape(2 * pairs, 3, 8, F)


def from_blocks(v):
    pairs = v.shape[0] // 2
    v = v.reshape(pairs, 2, 3, 8, F)
    x, y = v[:, 0, 2], v[:, 1, 2]
    low = low_rows(x.shape)
    a1 = jnp.where(low, x, pltpu.roll(y, 4, 1))
    b1 = jnp.where(low, pltpu.roll(x, 4, 1), y)
    re = jnp.stack([v[:, 0, 0], a1, v[:, 1, 0]], axis=1).reshape(pairs * 24, F)
    im = jnp.stack([v[:, 0, 1], b1, v[:, 1, 1]], axis=1).reshape(pairs * 24, F)
    return re, im


def far_first(n):
    return sorted(range(1, n), key=lambda o: -min(o, n - o))


def group_order(n):
    nx = min(4, n)
    hops = lambda j: 2 * (j // nx) + min(j % nx, nx - j % nx)
    back = [j // nx * nx + (nx - j % nx) % nx for j in range(n)]
    return nx, sorted(range(1, n), key=lambda j: -hops(j)), back


def slot_of(o, n):
    return 0 if o == 0 else 2 * o - 1 if o <= n // 2 else 2 * (n - o)


def kernel(
    zs, gs, feat_h, pos_h, wave_h, filt_h, mix_h, msgw_h, width_h, dist_h, nbr_h, gain_h, inw_h, outw_h, out,
    fall, halo, ut, pt, pcs, stage, acc, sc_buf, rc_buf, sz_buf, rz_buf,
    ysrc, yall, yv, es, er, msg_t, feat, pos, wave, filt, mix, msgw, width, dist, nbr, gain, inw, outw,
    know, in_s, ag_s, ag_r, ha_s, ha_r, c_s, c_r, z_s, z_r, zb_s, zb_r, yb_s, yb_r, e_s, e_r,
):
    f32, bf16 = jnp.float32, jnp.bfloat16
    dot = functools.partial(lax.dot_general, preferred_element_type=f32)
    me_s, me_g = lax.axis_index("space"), lax.axis_index("kgrp")
    z, yl, c = me_s // 4, lax.rem(me_s // 2, 2), lax.rem(me_s, 2)
    n_dev = 4 * zs * gs
    flat = me_s * gs + me_g
    up, down = lax.rem(flat + 1, n_dev), lax.rem(flat + n_dev - 1, n_dev)
    up = (up // gs, lax.rem(up, gs))
    down = (down // gs, lax.rem(down, gs))
    nx, group_far, group_back = group_order(gs)
    row, col = me_g // nx, lax.rem(me_g, nx)
    group = [(me_s, lax.rem(row + j // nx, gs // nx) * nx + lax.rem(col + j % nx, nx)) for j in range(gs)]
    core = (z * 4 + yl * 2 + 1 - c, me_g)
    ypeer = (z * 4 + (1 - yl) * 2 + c, me_g)
    diagonal = (z * 4 + (1 - yl) * 2 + 1 - c, me_g)
    ring_z = [lax.rem(z + o, zs) for o in range(zs)]
    ring = [(at * 4 + yl * 2 + c, me_g) for at in ring_z]
    offset_of = sorted(range(zs), key=lambda o: slot_of(o, zs))
    atoms = feat.shape[0]
    kw = wave.shape[1]
    rows = kw // 4

    def remote(src, dst, send, recv, device):
        return pltpu.make_async_remote_copy(
            src_ref=src, dst_ref=dst, send_sem=send, recv_sem=recv, device_id=device, device_id_type=MESH
        )

    def signal(sem, device):
        pl.semaphore_signal(sem, inc=1, device_id=device, device_id_type=MESH)

    barrier = pltpu.get_barrier_semaphore()
    peers = group[1:] + [up, down, core, ypeer, diagonal, ring[1], ring[zs - 1]]
    for device in peers:
        signal(barrier, device)

    pair = ((c * 2 + yl) * zs + z) // 2
    filt_part = filt_h.at[pl.ds(pl.multiple_of(pair * 24, 8), 24)]
    fetch = [
        pltpu.make_async_copy(src, dst, in_s.at[i])
        for i, (src, dst) in enumerate(
            (
                (pos_h, pos), (wave_h, wave), (feat_h, feat), (filt_part, filt), (mix_h, mix), (msgw_h, msgw),
                (width_h, width), (dist_h, dist), (nbr_h, nbr), (gain_h, gain), (inw_h, inw), (outw_h, outw),
            )
        )
    ]
    for copy in fetch:
        copy.start()
    fetch[0].wait()
    fetch[1].wait()

    turned = [pos[:, pl.ds(pl.multiple_of(at * atoms, atoms), atoms)] for _, at in group]
    scales = lax.broadcasted_iota(jnp.int32, pos.shape, 0)
    scales = jnp.where(scales < 2, 1.0 / BOX, 1.0 / (n_dev * atoms * SLAB_STEP)).astype(f32)
    pieces = split3(jnp.concatenate(turned, axis=1) * scales)
    counts = wave[...].astype(f32)
    counts = jnp.concatenate([counts, counts, counts], axis=0).astype(bf16)

    fetch[2].wait()
    pl.semaphore_wait(barrier, len(peers))

    for j in group_far:
        remote(feat, fall.at[group_back[j]], ag_s, ag_r, group[j]).start()
    edge = atoms // 4
    remote(feat.at[pl.ds(atoms - edge, edge)], halo.at[0], ha_s, ha_r, up).start()
    remote(feat.at[pl.ds(0, edge)], halo.at[1], ha_s, ha_r, down).start()
    fall[0] = feat[...]

    def received(ref, sem):
        remote(ref, ref, ag_s, sem, core).wait_recv()

    def sent(ref, sem):
        remote(ref, ref, sem, ag_r, core).wait_send()

    steps = []
    reach = 1
    while reach < zs // 2:
        steps.append(reach)
        reach *= 2

    def tell(i):
        if i < len(steps):
            signal(know.at[i], ring[steps[i]])
            signal(know.at[i], ring[zs - steps[i]])

    def hear(i):
        if i < len(steps):
            pl.semaphore_wait(know.at[i], 2)

    tell(0)

    chunk = 16 if rows % 16 == 0 else 8
    dom = gs * atoms
    ut[0:kw, 0:dom] = dot(counts, pieces, TN)

    @pl.loop(0, kw // chunk)
    def _(i):
        at = pl.ds(pl.multiple_of(i * chunk, chunk), chunk)
        cos_v, sin_v = cos_sin_turns(ut[at, 0:dom])
        quarter = i // (rows // chunk)
        at = pl.ds(pl.multiple_of(lax.rem(i, rows // chunk) * chunk, chunk), chunk)
        pt[quarter, 0, at, :] = cos_v.astype(bf16)
        pt[quarter, 1, at, :] = sin_v.astype(bf16)

    hear(0)
    tell(1)
    hear(1)
    tell(2)
    if gs > 1:
        received(fall.at[pl.ds(1, gs - 1)], ag_r)

    feats = fall[...].reshape(gs * atoms, F)

    def structure(core_at, y_at):
        sums = dot(pt[core_at * 2 + y_at].reshape(2 * rows, dom), feats, NN)
        stage[...] = to_blocks(sums[:rows], sums[rows:])
        return [stage[pl.ds(ring_z[o], 1)][0] for o in offset_of]

    cut = zs // 2
    cut = 11 if zs == 16 else cut
    parts = ((cut, zs), (0, cut))
    quad = (diagonal, ypeer, core)

    def swap(k, i):
        part = pl.ds(parts[i][0], parts[i][1] - parts[i][0])
        remote(sc_buf.at[k, part], rc_buf.at[k, part], c_s, c_r.at[i], quad[k]).start()

    for k, (core_at, y_at) in enumerate(((1 - c, 1 - yl), (c, 1 - yl), (1 - c, yl))):
        for s, v in enumerate(structure(core_at, y_at)):
            sc_buf[k, s] = v.astype(bf16)
        swap(k, 0)
        swap(k, 1)
    mine = structure(c, yl)
    hear(2)
    for i, (lo, hi) in enumerate(parts):
        received(rc_buf.at[:, pl.ds(lo, hi - lo)], c_r.at[i])
        for s in range(hi - 1, lo - 1, -1):
            total = mine[s]
            for k in range(3):
                total = total + rc_buf[k, s].astype(f32)
            if s == 0:
                acc[...] = total
                continue
            sz_buf[s] = total.astype(bf16)
            o = offset_of[s]
            remote(sz_buf.at[s], rz_buf.at[slot_of(zs - o, zs)], z_s, z_r, ring[o]).start()

    for copy in fetch[3:]:
        copy.wait()
    total = acc[...]
    others = pl.ds(1, zs - 1)
    received(rz_buf.at[others], z_r)
    for s in range(1, zs):
        total = total + rz_buf[s].astype(f32)

    a = (total * (1.0 / math.sqrt(n_dev * atoms))).reshape(24, F).astype(bf16)
    r0 = dot(a, mix[0], NN).reshape(3, 8, F)
    r1 = dot(a, mix[1], NN).reshape(3, 8, F)
    odd = lax.rem(z, 2) == 1
    fil = filt[...].reshape(3, 8, F)
    low = low_rows((8, F))
    swapped = pltpu.roll(fil[1], 4, 0)
    f_main = jnp.where(odd, fil[2], fil[0])
    f_mixed = jnp.where(jnp.logical_xor(low, odd), fil[1], swapped)
    r1_swapped = pltpu.roll(r1[2], 4, 0)
    y_val = jnp.stack(
        [
            f_main * (r0[0] - r1[1]),
            f_main * (r1[0] + r0[1]),
            f_mixed * jnp.where(low, r0[2] - r1_swapped, r0[2] + r1_swapped),
        ],
        axis=0,
    ).astype(bf16)
    ysrc[...] = y_val
    here = c * 2 + yl
    cuts = (0, 5, 9, 13, 16) if zs == 16 else (0, zs // 2, zs)
    for o in far_first(zs):
        s = slot_of(zs - o, zs)
        part = sum(s >= hi for hi in cuts[1:])
        remote(ysrc, yall.at[here, s], zb_s, zb_r.at[part], ring[o]).start()
    yall[pl.ds(here, 1), 0] = y_val[None]

    send_order = group_far + [0]
    lanes = [pieces[:, j * atoms : (j + 1) * atoms] for j in send_order]
    ut[0:dom, 0:kw] = dot(jnp.concatenate(lanes, axis=1), counts, TN)

    @pl.loop(0, dom // 16)
    def _(i):
        at = pl.ds(pl.multiple_of(i * 16, 16), 16)
        cos_v, sin_v = cos_sin_turns(ut[at, 0:kw])
        pcs[at, 0:kw] = cos_v.astype(bf16)
        pcs[at, kw : 2 * kw] = sin_v.astype(bf16)

    received(halo, ha_r)
    weight = msgw[...]
    ext = jnp.concatenate(
        [
            dot(halo[0], weight, NN),
            dot(feat[...], weight, NN),
            dot(halo[1], weight, NN),
            jnp.zeros((edge * 2, F), f32),
        ],
        axis=0,
    )
    ext_t = ext.T.astype(bf16)
    inv_width = (1.0 / jnp.broadcast_to(width[...], (F, F))).T
    row_ids = lax.broadcasted_iota(jnp.int32, (2 * atoms, atoms), 0)
    message = jnp.zeros((F, atoms), f32)
    for j in range(nbr.shape[0]):
        hot = jnp.where(row_ids == nbr[j : j + 1, :], 1.0, 0.0).astype(bf16)
        near = dot(ext_t, hot, NN)
        message = message + jnp.exp(-(dist[j : j + 1, :] * inv_width)) * near
    msg_t[...] = message.T

    for i in range(len(cuts) - 1):
        lo, hi = cuts[i], cuts[i + 1]
        if hi > max(lo, 1):
            received(yall.at[here, pl.ds(max(lo, 1), hi - max(lo, 1))], zb_r.at[i])
        here_part = yall.at[here, pl.ds(lo, hi - lo)]
        for device in (diagonal, ypeer, core):
            remote(here_part, here_part, yb_s, yb_r, device).start()
    received(yall.at[pl.ds(1, 3)], yb_r)

    slots = []
    for t in range(zs):
        o = lax.rem(t - z + zs, zs)
        slots.append(jnp.where(o <= zs // 2, jnp.maximum(2 * o - 1, 0), 2 * (zs - o)))
    for q in range(4):
        blocks = [yall[q, pl.ds(slots[t], 1)] for t in range(zs)]
        re, im = from_blocks(jnp.concatenate(blocks, axis=0).astype(f32))
        yv[q * rows : (q + 1) * rows, :] = re.astype(bf16)
        yv[kw + q * rows : kw + (q + 1) * rows, :] = im.astype(bf16)
    inv_scale = 1.0 / math.sqrt(kw * gs)

    bounds = (0, 1, 4, 8) if gs == 8 else (0, gs)
    for lo, hi in zip(bounds[:-1], bounds[1:]):
        terms = dot(pcs[lo * atoms : hi * atoms, :], yv[...], NN) * inv_scale
        for i in range(lo, hi):
            j = send_order[i]
            term = terms[(i - lo) * atoms : (i - lo + 1) * atoms]
            if j == 0:
                ewald = term
                continue
            es[j] = term.astype(bf16)
            remote(es.at[j], er.at[group_back[j]], e_s, e_r, group[j]).start()

    sent(halo, ha_s)
    sent(sc_buf, c_s)
    sent(sz_buf.at[others], z_s)
    sent(yall.at[here, others], zb_s)
    sent(yall.at[pl.ds(1, 3)], yb_s)
    if gs > 1:
        rest = pl.ds(1, gs - 1)
        sent(fall.at[rest], ag_s)
        received(er.at[rest], e_r)
        sent(es.at[rest], e_s)
    for o in range(1, gs):
        ewald = ewald + er[o].astype(f32)

    mixed = feat[...].astype(f32) + msg_t[...] + ewald
    inverse = lax.rsqrt(jnp.mean(mixed * mixed, axis=1, keepdims=True) + 1e-06)
    normed = (mixed * inverse * gain[...]).astype(bf16)
    pre = dot(normed, inw[...], NN)
    hidden = (pre * (1.0 / (1.0 + jnp.exp(-pre)))).astype(bf16)
    out[...] = (mixed + dot(hidden, outw[...], NN)).astype(bf16)


def solution(mesh):
    zs, gs = mesh.shape["space"] // 4, mesh.shape["kgrp"]

    def local(features, positions, wave_index, wave_filter, mix_pair, msg_weight, chan_width, pair_dist,
              neighbours, norm_gain, in_weight, out_weight):
        atoms = features.shape[0]
        dom = gs * atoms
        kw = wave_index.shape[0]
        f32, bf16 = jnp.float32, jnp.bfloat16
        blk = (3, 8, F)
        big = max(kw, dom)
        vm = pltpu.VMEM
        dma = pltpu.SemaphoreType.DMA
        scratch = [
            vm((gs, atoms, F), bf16),
            vm((2, atoms // 4, F), bf16),
            vm((big, big), f32),
            vm((4, 2, kw // 4, dom), bf16),
            vm((dom, 2 * kw), bf16),
            vm((zs, *blk), f32),
            vm(blk, f32),
            vm((3, zs, *blk), bf16),
            vm((3, zs, *blk), bf16),
            vm((zs, *blk), bf16),
            vm((zs, *blk), bf16),
            vm(blk, bf16),
            vm((4, zs, *blk), bf16),
            vm((2 * kw, F), bf16),
            vm((gs, atoms, F), bf16),
            vm((gs, atoms, F), bf16),
            vm((atoms, F), f32),
            vm((atoms, F), bf16),
            vm((3, dom), f32),
            vm((3, kw), jnp.int32),
            vm((2 * WB, F), f32),
            vm(mix_pair.shape, bf16),
            vm(msg_weight.shape, bf16),
            vm((1, F), f32),
            vm(pair_dist.shape[::-1], f32),
            vm(neighbours.shape[::-1], jnp.int32),
            vm((1, F), f32),
            vm(in_weight.shape, bf16),
            vm(out_weight.shape, bf16),
            pltpu.SemaphoreType.REGULAR((3,)),
            dma((12,)),
            dma, dma, dma, dma,
            dma, dma((2,)),
            dma, dma, dma, dma((4,)),
            dma, dma, dma, dma,
        ]
        return pl.pallas_call(
            functools.partial(kernel, zs, gs),
            out_shape=jax.ShapeDtypeStruct((atoms, F), bf16),
            in_specs=[pl.BlockSpec(memory_space=pl.ANY)] * 12,
            out_specs=pl.BlockSpec(memory_space=pltpu.VMEM),
            scratch_shapes=scratch,
            compiler_params=pltpu.CompilerParams(
                collective_id=0, has_side_effects=True, vmem_limit_bytes=60 * 1024 * 1024
            ),
        )(
            features, positions.T, wave_index.T, wave_filter, mix_pair, msg_weight,
            chan_width.reshape(1, F), pair_dist.T, neighbours.T, norm_gain.reshape(1, F), in_weight, out_weight,
        )

    placed = (
        P(("space", "kgrp"), None), P("space", None), P("kgrp", None), P("kgrp", None), P(), P(), P(),
        P(("space", "kgrp"), None), P(("space", "kgrp"), None), P(), P(), P(),
    )
    return jax.shard_map(
        local, mesh=mesh, in_specs=placed, out_specs=P(("space", "kgrp"), None), check_vma=False
    )
```
